32 devices in a mesh: groups: 2 (over x), seq: 16 (over z, y, core).
Axes of the slice: x: 2, y: 2, z: 4, core: 2. Of those that a mesh axis runs over, the one named last changes fastest.
Arguments:
- queries: bfloat16 [4096, 2560], P(('groups', 'seq')), parts along dimension 0, may hold values from -12 to 12
- key_vectors: bfloat16 [4096, 2560], P(('groups', 'seq')), parts along dimension 0, may hold values from -6 to 6
- value_vectors: bfloat16 [4096, 2560], P(('groups', 'seq')), parts along dimension 0, may hold values from -6 to 6
- step_sizes: float32 [4096, 8], P(('groups', 'seq')), parts along dimension 0, may hold values from 0.02 to 0.3
- fast_weights: float32 [320, 7680], P('seq'), may hold values from -20 to 20
- fast_gain: float32 [2560], replicated, may hold values from 0.25 to 1.75
- window_gain: float32 [2560], replicated, may hold values from 0.25 to 1.75
Outputs:
- layer_out: bfloat16 [4096, 2560], P(('groups', 'seq')), parts along dimension 0
- new_weights: float32 [640, 7680], P(('groups', 'seq')), parts along dimension 0
- momentum: float32 [640, 7680], P(('groups', 'seq')), parts along dimension 0
The draws below stay inside these ranges and needn't reach their ends.
There are 2 independent parts, one for each index of `groups`. The reference program is written for one: setup_inputs(seed, part) draws one part's arguments, and reference() takes and returns one part's arrays. A program takes and returns all parts, laid end to end along the dimension named above; an argument that names none is the same for every part. Nothing has to cross between parts.
All inputs are finite; a program needn't handle non-finite values.
Results may differ from the reference program's by a relative error of at most 0.0066.
Values may be sent and summed in bfloat16 or wider, within the bound.
A program may use at most 128 MiB of HBM per device.

```python
import math
import jax
import jax.numpy as jnp
from jax import lax

H = 8
DH = 320
WINDOW = 1024
BLOCK = 2048


def draw_queries(key, part):
    return jnp.clip(jax.random.normal(jax.random.fold_in(key, 1), (BLOCK, H * DH)), -6.0, 6.0).astype(jnp.bfloat16)


def draw_key_vectors(key, part):
    return jnp.clip(jax.random.normal(jax.random.fold_in(key, 2), (BLOCK, H * DH)), -6.0, 6.0).astype(jnp.bfloat16)


def draw_fast_weights(key, part):
    columns = 3 * H * DH
    rising = (3.0 ** (jnp.arange(DH, dtype=jnp.float32) / (DH - 1)))[:, None]
    entries = jnp.clip(jax.random.normal(jax.random.fold_in(key, 1), (DH, columns)), -4.0, 4.0)
    row_factor = 0.5 * rising * jnp.exp(jax.random.uniform(jax.random.fold_in(key, 2), (DH, 1), minval=-0.7, maxval=0.7))
    col_factor = jnp.exp(jax.random.uniform(jax.random.fold_in(key, 3), (1, columns), minval=-1.15, maxval=1.15))
    return jnp.clip(entries * row_factor * col_factor, -20.0, 20.0)


def shard_levels(rng, shape, shards, smallest, largest):
    def one(position, parts):
        steps = jax.random.uniform(jax.random.fold_in(jax.random.fold_in(rng, 6), position), (parts,), jnp.float32, smallest / len(shards), largest / len(shards))
        return jnp.repeat(jnp.exp(steps), shape[position] // parts).reshape((-1,) + (1,) * (len(shape) - position - 1))

    factor_of = one(*shards[0])
    for cut in shards[1:]:
        factor_of = factor_of * one(*cut)
    return factor_of


def gaussian(key, dims, deviation, reach, split=(), kind=jnp.bfloat16):
    values = deviation * jax.random.normal(key, dims, jnp.float32)
    if split:
        values = values * shard_levels(key, dims, split, -0.22, 0.18)
    return jnp.clip(values, -reach, reach).astype(kind)


def setup_inputs(seed: int = 0, part: int = 0) -> dict:
    key_list = jax.random.split(jax.random.key(seed), 8)
    own_keys = jax.random.split(jax.random.fold_in(key_list[7], part), 8)
    return {
        "queries": draw_queries(jax.random.fold_in(jax.random.fold_in(key_list[7], part), 71), part),
        "key_vectors": draw_key_vectors(jax.random.fold_in(jax.random.fold_in(key_list[7], part), 71), part),
        "value_vectors": gaussian(own_keys[2], (BLOCK, H * DH), 1.0, 6.0, ((0, 16),)),
        "step_sizes": jnp.clip(jnp.exp(math.log(0.3) - 2.7080503 * jax.random.uniform(own_keys[3], (BLOCK, H), jnp.float32) ** shard_levels(own_keys[3], (BLOCK, H), ((0, 16),), -0.2, 0.2)), 0.02, 0.3),
        "fast_weights": draw_fast_weights(jax.random.fold_in(key_list[7], 71), part),
        "fast_gain": jnp.clip(1.0 + 0.15 * jax.random.normal(key_list[5], (H * DH,), jnp.float32), 0.25, 1.75),
        "window_gain": jnp.clip(1.0 + 0.15 * jax.random.normal(key_list[6], (H * DH,), jnp.float32), 0.25, 1.75),
    }


def normalize(field, gain_row):
    mean_sq = lax.optimization_barrier(jnp.mean(field * field, axis=-1, keepdims=True))
    return field * lax.rsqrt(mean_sq + 1e-05) * gain_row

def silu_slope(gate):
    sigma = jax.nn.sigmoid(gate)
    return sigma * (1.0 + gate * (1.0 - sigma))

def reference(queries, key_vectors, value_vectors, step_sizes, fast_weights, fast_gain, window_gain):
    score_scale = 1.0 / math.sqrt(DH)
    copies = fast_weights.astype(jnp.bfloat16).reshape(DH, 3, H, DH)
    w_first = copies[:, 0]
    w_third = copies[:, 1]
    w_second = copies[:, 2]
    query_heads = queries.reshape(BLOCK, H, DH)
    key_heads = key_vectors.reshape(BLOCK, H, DH)
    value_heads = value_vectors.reshape(BLOCK, H, DH)

    def project(inputs, matrix):
        return jnp.einsum('thr,rhc->thc', inputs.astype(jnp.float32), matrix.astype(jnp.float32)) * score_scale
    gate_query = project(query_heads, w_first)
    up_query = project(query_heads, w_third)
    hidden_query = (jax.nn.silu(gate_query) * up_query).astype(jnp.bfloat16)
    fast_part = normalize(project(hidden_query, w_second), fast_gain.reshape(H, DH))
    padding = jnp.zeros((WINDOW, H * DH), jnp.bfloat16)
    padded_keys = jnp.concatenate([padding, key_vectors], axis=0)
    padded_values = jnp.concatenate([padding, value_vectors], axis=0)

    def window_block(block_index):
        begin = block_index * WINDOW
        query_block = lax.dynamic_slice_in_dim(queries, begin, WINDOW, 0).reshape(WINDOW, H, DH)
        key_block = lax.dynamic_slice_in_dim(padded_keys, begin, 2 * WINDOW, 0).reshape(2 * WINDOW, H, DH)
        value_block = lax.dynamic_slice_in_dim(padded_values, begin, 2 * WINDOW, 0).reshape(2 * WINDOW, H, DH)
        query_pos = begin + jnp.arange(WINDOW, dtype=jnp.int32)
        key_pos = begin - WINDOW + jnp.arange(2 * WINDOW, dtype=jnp.int32)
        distance = query_pos[:, None] - key_pos[None, :]
        allowed = (distance >= 0) & (distance < WINDOW) & (key_pos[None, :] >= 0)
        scores = jnp.einsum('qhd,khd->hqk', query_block.astype(jnp.float32), key_block.astype(jnp.float32)) * score_scale
        scores = jnp.where(allowed[None], scores, -jnp.inf)
        row_max = lax.optimization_barrier(jnp.max(scores, axis=-1, keepdims=True))
        weights = jnp.exp(scores - row_max)
        attention_probs = (weights / lax.optimization_barrier(jnp.sum(weights, axis=-1, keepdims=True))).astype(jnp.bfloat16)
        return jnp.einsum('hqk,khd->qhd', attention_probs.astype(jnp.float32), value_block.astype(jnp.float32))
    attended = lax.map(window_block, jnp.arange(BLOCK // WINDOW, dtype=jnp.int32)).reshape(BLOCK, H, DH)
    window_part = normalize(attended, window_gain.reshape(H, DH))
    layer_out = (fast_part + window_part).astype(jnp.bfloat16).reshape(BLOCK, H * DH)
    gate_key = project(key_heads, w_first)
    up_key = project(key_heads, w_third)
    hidden_key = (jax.nn.silu(gate_key) * up_key).astype(jnp.bfloat16)
    target = (-step_sizes[:, :, None] * value_heads.astype(jnp.float32)).astype(jnp.bfloat16)
    back_hidden = jnp.einsum('thc,rhc->thr', target.astype(jnp.float32), w_second.astype(jnp.float32)) * score_scale
    grad_gate = (back_hidden * up_key * silu_slope(gate_key)).astype(jnp.bfloat16)
    grad_up = (back_hidden * jax.nn.silu(gate_key)).astype(jnp.bfloat16)
    key_float = key_heads.astype(jnp.float32)
    first = jnp.einsum('thr,thc->rhc', key_float, grad_gate.astype(jnp.float32))
    third = jnp.einsum('thr,thc->rhc', key_float, grad_up.astype(jnp.float32))
    second = jnp.einsum('thr,thc->rhc', hidden_key.astype(jnp.float32), target.astype(jnp.float32))
    momentum = jnp.stack([first, third, second], axis=1).reshape(DH, 3 * H * DH) * score_scale
    moved = fast_weights - momentum
    old_sum = lax.optimization_barrier(jnp.sum(fast_weights * fast_weights, axis=0))
    new_sum = lax.optimization_barrier(jnp.sum(moved * moved, axis=0))
    new_weights = moved * jnp.sqrt((old_sum + 1e-06) / (new_sum + 1e-06))
    return (layer_out, new_weights, momentum)
```

```python
import functools
import math

import jax
import jax.numpy as jnp
from jax import lax
from jax.experimental import pallas as pl
from jax.experimental.pallas import tpu as pltpu
from jax.sharding import PartitionSpec as P

WINDOW = 1024
LANES = 128
F32 = jnp.float32
BF16 = jnp.bfloat16


def dot(a, b):
    return jnp.dot(a, b, preferred_element_type=F32)


def dot_nt(a, b):
    return lax.dot_general(a, b, (((1,), (1,)), ((), ())), preferred_element_type=F32)


def dot_tn(a, b):
    return lax.dot_general(a, b, (((0,), (0,)), ((), ())), preferred_element_type=F32)


def kernel(
    n, groups, heads, width,
    kvq_in, step_in, w_in, gains,
    out, g_out, scale_out,
    kv, qb, qx, stb, wb, wfull, kn, vt, hid, tgt, gg, gu,
    gstage, gother, ginc, gsend, sums, sinc, scale_send, ostage, gain_rows,
    own_o, own_l, fast_o, xo_stage, xl_stage, xo, xl,
    s_in, r_k, r_v, r_q, r_x, r_st, r_w,
    s_wf, s_x, s_xo, s_xl, r_xo, r_xl,
    s_gp, r_gp, s_sp, r_sp, s_g, r_g, s_sc, r_sc, s_o, r_o,
):
    group = n // heads
    rows = width // n
    span = heads * LANES
    scale = 1.0 / math.sqrt(width)
    me = lax.axis_index("seq")
    part = lax.axis_index("groups")
    head = me % heads
    member = me // heads

    def remote(src, dst, send, recv, device, to_part=None):
        return pltpu.make_async_remote_copy(
            src_ref=src, dst_ref=dst, send_sem=send, recv_sem=recv,
            device_id={"groups": part if to_part is None else to_part, "seq": device},
            device_id_type=pl.DeviceIdType.MESH,
        )

    barrier = pltpu.get_barrier_semaphore()
    for step in range(1, n):
        pl.semaphore_signal(
            barrier, inc=1, device_id={"seq": lax.rem(me + step, n)},
            device_id_type=pl.DeviceIdType.MESH,
        )
    for other in range(1, groups):
        for d in range(group):
            pl.semaphore_signal(
                barrier, inc=1,
                device_id={"groups": lax.rem(part + other, groups), "seq": d * heads + head},
                device_id_type=pl.DeviceIdType.MESH,
            )
    pl.semaphore_wait(barrier, n - 1 + (groups - 1) * group)

    def head_rows(which):
        return pl.ds(pl.multiple_of(which * width, 64), width)

    pending = []
    base = member * heads
    below = member < group - 1
    above = member > 0

    def spread(src_of, dst, recv, kind):
        for step in range(heads):
            which = lax.rem(head + step, heads)
            src = src_of(which)
            if step == 0:
                pltpu.make_async_copy(src, dst, recv).start()
            else:
                copy = remote(src, dst, s_in.at[kind, step], recv, base + which)
                copy.start()
                pending.append(copy)

    stride = heads // groups
    shift = lax.rem(part + groups * heads - 2 * head, groups)
    w_maybe = []
    for step in range(stride):
        offset = shift + groups * step
        which = lax.rem(head + offset, heads)
        copy = remote(w_in.at[which], wb.at[me], s_in.at[4, step], r_w.at[me], base + which)
        if step == 0:
            @pl.when(offset == 0)
            def _():
                pltpu.make_async_copy(w_in.at[which], wb.at[me], r_w.at[me]).start()

            @pl.when(offset != 0)
            def _():
                copy.start()
            w_maybe.append(copy)
        else:
            copy.start()
            pending.append(copy)
    spread(lambda w: kvq_in.at[w, 0], kv.at[head, 0], r_k.at[head], 0)
    crossing = []
    for step in range(heads):
        which = lax.rem(head + step, heads)
        copy = remote(
            kvq_in.at[which, 2], qx.at[head], s_x.at[step], r_x.at[head],
            jnp.maximum(member - 1, 0) * heads + which,
        )
        crossing.append(copy)

        @pl.when(above)
        def _():
            copy.start()
    spread(lambda w: kvq_in.at[w, 1], kv.at[head, 1], r_v.at[head], 1)
    spread(lambda w: step_in, stb.at[head], r_st.at[head], 2)
    spread(lambda w: kvq_in.at[w, 2], qb.at[head], r_q.at[head], 3)

    def landed(ref, sem):
        pltpu.make_async_copy(ref, ref, sem).wait()

    for h in range(heads):
        @pl.when(head == h)
        def _():
            at = slice(h * width, (h + 1) * width)
            gain_rows[0] = jnp.broadcast_to(gains[0:1, at], (8, width))
            gain_rows[1] = jnp.broadcast_to(gains[1:2, at], (8, width))

    first = lax.rem(part + groups * heads - head, groups)
    for t in range(stride):
        slot = base + first + groups * t
        landed(wb.at[slot], r_w.at[slot])
        for other in range(groups):
            for d in range(group):
                if other + d == 0:
                    continue
                copy = remote(
                    wb.at[slot], wb.at[slot], s_wf.at[t, other * group + d], r_w.at[slot],
                    lax.rem(member + d, group) * heads + head, lax.rem(part + other, groups),
                )
                copy.start()
                pending.append(copy)

    for i in range(heads):
        landed(kv.at[i, 0], r_k.at[i])
        kn[i * LANES : (i + 1) * LANES, :] = kv[i, 0].T
    for i in range(heads):
        landed(kv.at[i, 1], r_v.at[i])
        vt[:, i * LANES : (i + 1) * LANES] = kv[i, 1]

    chunk = 2 * LANES
    key_at = lax.broadcasted_iota(jnp.int32, (span, chunk), 0)
    lane_at = lax.broadcasted_iota(jnp.int32, (1, chunk), 1)

    def soften(scores, values):
        top = jnp.max(scores, axis=0, keepdims=True)
        weights = jnp.exp(scores - top)
        total = jnp.sum(weights, axis=0, keepdims=True)
        probs = (weights * (1.0 / total)).astype(BF16)
        return dot(values, probs), top + jnp.log(total)

    def cross(step, carry):
        slots = [lax.rem(head + heads - 2 * step - half, heads) for half in range(2)]
        for slot in slots:
            landed(qx.at[slot], r_x.at[slot])
        query = jnp.concatenate([qx[slot] for slot in slots], axis=1)
        at = jnp.where(lane_at < LANES, slots[0] * LANES + lane_at, slots[1] * LANES + lane_at - LANES)
        scores = jnp.where(key_at > at, dot(kn[...], query) * scale, -1e30)
        field, level = soften(scores, vt[...])
        field = field.astype(BF16)
        level = jnp.broadcast_to(level, (8, chunk))
        for half, slot in enumerate(slots):
            there = slice(half * LANES, (half + 1) * LANES)
            xo_stage[slot] = field[:, there]
            xl_stage[slot] = level[:, there]
            remote(xo_stage.at[slot], xo.at[slot], s_xo.at[slot], r_xo.at[slot], me + heads).start()
            remote(xl_stage.at[slot], xl.at[slot], s_xl.at[slot], r_xl.at[slot], me + heads).start()
        return carry

    @pl.when(below)
    def _():
        lax.fori_loop(0, heads // 4, cross, 0)

    for d in range(group):
        for e in range(groups):
            if d + e == 0:
                continue
            for t in range(stride):
                slot = lax.rem(member + d, group) * heads + lax.rem(first + e, groups) + groups * t
                landed(wb.at[slot], r_w.at[slot])
    for s in range(n):
        piece = wb[s].astype(F32)
        for m in range(3):
            wfull[m, s * rows : (s + 1) * rows, :] = piece[m * rows : (m + 1) * rows, :]
    for i in range(heads):
        landed(stb.at[i], r_st.at[i])

    w1 = wfull[0].astype(BF16)
    w3 = wfull[1].astype(BF16)
    w2 = wfull[2].astype(BF16)

    for i in range(heads):
        there = pl.ds(i * LANES, LANES)
        tgt[:, there] = (-stb[i, pl.ds(head, 1), :] * kv[i, 1].astype(F32)).astype(BF16)

    def grad_chunk(c, carry):
        there = pl.ds(pl.multiple_of(c * chunk, chunk), chunk)
        keys = jnp.concatenate([kv[2 * c, 0], kv[2 * c + 1, 0]], axis=1)
        gate = dot_tn(w1, keys) * scale
        up = dot_tn(w3, keys) * scale
        back = dot(w2, tgt[:, there]) * scale
        sigma = jax.nn.sigmoid(gate)
        silu = gate * sigma
        hid[:, there] = (silu * up).astype(BF16)
        gg[:, there] = (back * up * (sigma * (1.0 + gate * (1.0 - sigma)))).astype(BF16)
        gu[:, there] = (back * silu).astype(BF16)
        return carry

    lax.fori_loop(0, span // chunk, grad_chunk, 0)
    own_keys = jnp.concatenate([kv[i, 0] for i in range(heads)], axis=1)
    for m, (left, right) in enumerate(((own_keys, gg), (own_keys, gu), (hid[...], tgt))):
        grad = dot_nt(left, right[...]) * scale
        for s in range(n):
            gstage[s // heads, s % heads, m * rows : (m + 1) * rows, :] = grad[s * rows : (s + 1) * rows, :]

    for d in range(1, group):
        other = lax.rem(member + d, group)
        for i in range(heads):
            gother[d - 1, i] = gstage[other, i].astype(BF16)
        copy = remote(gother.at[d - 1], ginc.at[d - 1], s_gp.at[d - 1], r_gp.at[d - 1], other * heads + head)
        copy.start()
        pending.append(copy)

    @pl.when(below)
    def _():
        lax.fori_loop(heads // 4, heads // 2, cross, 0)

    fast_column = gain_rows[0].T[:, 0:1]
    window_column = gain_rows[1].T[:, 0:1]

    def normalize(field, gain):
        mean_sq = jnp.mean(field * field, axis=0, keepdims=True)
        return field * lax.rsqrt(mean_sq + 1e-05) * gain

    def attend(c):
        reach = (c + 1) * chunk
        query = jnp.concatenate([qb[2 * c], qb[2 * c + 1]], axis=1)
        scores = dot(kn[:reach, :], query) * scale
        scores = jnp.where(key_at[:reach] <= lane_at + c * chunk, scores, -1e30)
        attended, level = soften(scores, vt[:, :reach])
        level = jnp.broadcast_to(level, (8, chunk))
        gate = dot_tn(w1, query) * scale
        up = dot_tn(w3, query) * scale
        hidden = (gate * jax.nn.sigmoid(gate) * up).astype(BF16)
        fast_part = normalize(dot_tn(w2, hidden) * scale, fast_column)
        for half in range(2):
            there = slice(half * LANES, (half + 1) * LANES)
            own_o[2 * c + half] = attended[:, there]
            own_l[2 * c + half] = level[:, there]
            fast_o[2 * c + half] = fast_part[:, there]

    for i in range(heads):
        landed(qb.at[i], r_q.at[i])
    for c in range(span // chunk):
        attend(c)

    for d in range(1, group):
        landed(ginc.at[d - 1], r_gp.at[d - 1])
    sums[...] = jnp.zeros_like(sums)

    def add_up(i, carry):
        total = gstage[member, i]
        for d in range(1, group):
            total = total + ginc[d - 1, i].astype(F32)
        gsend[i] = total.astype(BF16)
        weight = wb[base + i].astype(F32)
        moved = weight - total
        for m in range(3):
            piece = slice(m * rows, (m + 1) * rows)
            old = weight[piece, :]
            new = moved[piece, :]
            sums[m : m + 1, :] += jnp.sum(old * old, axis=0, keepdims=True)
            sums[4 + m : 5 + m, :] += jnp.sum(new * new, axis=0, keepdims=True)
        return carry

    lax.fori_loop(0, heads, add_up, 0)
    for d in range(1, group):
        copy = remote(
            sums, sinc.at[d - 1], s_sp.at[d - 1], r_sp.at[d - 1],
            lax.rem(member + d, group) * heads + head,
        )
        copy.start()
        pending.append(copy)
    for step in range(heads):
        i = lax.rem(head + step, heads)
        if step == 0:
            pltpu.make_async_copy(gsend.at[i], g_out.at[head], r_g.at[head]).start()
        else:
            copy = remote(gsend.at[i], g_out.at[head], s_g.at[step], r_g.at[head], base + i)
            copy.start()
            pending.append(copy)

    def finalize(step, carry):
        slot = lax.rem(head + heads - step, heads)

        @pl.when(above)
        def _():
            landed(xo.at[slot], r_xo.at[slot])
            landed(xl.at[slot], r_xl.at[slot])
            here = own_l[slot, 0:1, :]
            there = xl[slot, 0:1, :]
            share = 1.0 / (1.0 + jnp.exp(there - here))
            rest = 1.0 / (1.0 + jnp.exp(here - there))
            own_o[slot] = own_o[slot] * share + xo[slot].astype(F32) * rest

        result = (fast_o[slot] + normalize(own_o[slot], window_column)).astype(BF16)
        ostage[slot] = result
        dst = out.at[head_rows(head), :]

        @pl.when(step == 0)
        def _():
            pltpu.make_async_copy(ostage.at[slot], dst, r_o.at[head]).start()

        @pl.when(step != 0)
        def _():
            remote(ostage.at[slot], dst, s_o.at[slot], r_o.at[head], base + slot).start()
        return carry

    lax.fori_loop(0, heads // 2, finalize, 0)

    for d in range(1, group):
        landed(sinc.at[d - 1], r_sp.at[d - 1])
    total = sums[...]
    for d in range(1, group):
        total = total + sinc[d - 1]
    scale_send[0:4, :] = jnp.sqrt((total[0:4] + 1e-06) / (total[4:8] + 1e-06))
    scale_send[4:8, :] = total[4:8]
    for step in range(heads):
        i = lax.rem(head + step, heads)
        if step == 0:
            pltpu.make_async_copy(scale_send, scale_out.at[head], r_sc.at[head]).start()
        else:
            copy = remote(scale_send, scale_out.at[head], s_sc.at[step], r_sc.at[head], base + i)
            copy.start()
            pending.append(copy)

    lax.fori_loop(heads // 2, heads, finalize, 0)

    for i in range(heads):
        landed(g_out.at[i], r_g.at[i])
        landed(scale_out.at[i], r_sc.at[i])
        landed(out.at[pl.ds(i * width, width), :], r_o.at[i])
    for copy in pending:
        copy.wait_send()

    @pl.when(shift != 0)
    def _():
        for copy in w_maybe:
            copy.wait_send()

    @pl.when(above)
    def _():
        for copy in crossing:
            copy.wait_send()

    @pl.when(below)
    def _():
        for i in range(heads):
            remote(xo_stage.at[i], xo.at[i], s_xo.at[i], r_xo.at[i], me + heads).wait_send()
            remote(xl_stage.at[i], xl.at[i], s_xl.at[i], r_xl.at[i], me + heads).wait_send()

    for step in range(1, heads):
        slot = lax.rem(head + heads - step, heads)
        remote(ostage.at[slot], out.at[head_rows(head), :], s_o.at[slot], r_o.at[head], base + slot).wait_send()


def prepare(heads, width, rows, k, v, q, weights, kvq, pieces, wide):
    for m, ref in enumerate((k, v, q)):
        flipped = ref[...].T
        for h in range(heads):
            kvq[h, m] = flipped[h * width : (h + 1) * width]
    for h in range(heads):
        for m in range(3):
            at = (m * heads + h) * width
            wide[h, m * rows : (m + 1) * rows, :] = weights[:, at : at + width]
        pieces[h] = wide[h].astype(BF16)


def finish(heads, width, rows, out_t, grads, scales, weights, layer_out, new_weights, momentum):
    layer_out[...] = out_t[...].T
    for h in range(heads):
        grad = grads[h].astype(F32)
        for m in range(3):
            at = (m * heads + h) * width
            part = grad[m * rows : (m + 1) * rows, :]
            momentum[:, at : at + width] = part
            new_weights[:, at : at + width] = (weights[:, at : at + width] - part) * scales[h, m : m + 1, :]


def shards(queries, key_vectors, value_vectors, step_sizes, fast_weights, fast_gain, window_gain):
    tokens = queries.shape[0]
    heads = step_sizes.shape[1]
    width = queries.shape[1] // heads
    n = lax.axis_size("seq")
    groups = lax.axis_size("groups")
    group = n // heads
    rows = width // n
    assert tokens == LANES and heads * tokens == WINDOW
    span = heads * LANES
    vmem = pl.BlockSpec(memory_space=pltpu.VMEM)
    dma = pltpu.SemaphoreType.DMA
    more = max(group - 1, 1)
    kvq, pieces = pl.pallas_call(
        functools.partial(prepare, heads, width, rows),
        out_shape=(
            jax.ShapeDtypeStruct((heads, 3, width, LANES), BF16),
            jax.ShapeDtypeStruct((heads, 3 * rows, width), BF16),
        ),
        in_specs=[vmem] * 4,
        out_specs=(vmem, vmem),
        scratch_shapes=[pltpu.VMEM((heads, 3 * rows, width), F32)],
        name="prepare",
    )(key_vectors, value_vectors, queries, fast_weights)
    out_t, grads, scales = pl.pallas_call(
        functools.partial(kernel, n, groups, heads, width),
        out_shape=(
            jax.ShapeDtypeStruct((heads * width, LANES), BF16),
            jax.ShapeDtypeStruct((heads, 3 * rows, width), BF16),
            jax.ShapeDtypeStruct((heads, 8, width), F32),
        ),
        in_specs=[vmem] * 4,
        out_specs=(vmem, vmem, vmem),
        scratch_shapes=[
            pltpu.VMEM((heads, 2, width, LANES), BF16),
            pltpu.VMEM((heads, width, LANES), BF16),
            pltpu.VMEM((heads, width, LANES), BF16),
            pltpu.VMEM((heads, heads, LANES), F32),
            pltpu.VMEM((n, 3 * rows, width), BF16),
            pltpu.VMEM((3, width, width), F32),
            pltpu.VMEM((span, width), BF16),
            pltpu.VMEM((width, span), BF16),
            pltpu.VMEM((width, span), BF16),
            pltpu.VMEM((width, span), BF16),
            pltpu.VMEM((width, span), BF16),
            pltpu.VMEM((width, span), BF16),
            pltpu.VMEM((group, heads, 3 * rows, width), F32),
            pltpu.VMEM((more, heads, 3 * rows, width), BF16),
            pltpu.VMEM((more, heads, 3 * rows, width), BF16),
            pltpu.VMEM((heads, 3 * rows, width), BF16),
            pltpu.VMEM((8, width), F32),
            pltpu.VMEM((more, 8, width), F32),
            pltpu.VMEM((8, width), F32),
            pltpu.VMEM((heads, width, LANES), BF16),
            pltpu.VMEM((2, 8, width), F32),
            pltpu.VMEM((heads, width, LANES), F32),
            pltpu.VMEM((heads, 8, LANES), F32),
            pltpu.VMEM((heads, width, LANES), F32),
            pltpu.VMEM((heads, width, LANES), BF16),
            pltpu.VMEM((heads, 8, LANES), F32),
            pltpu.VMEM((heads, width, LANES), BF16),
            pltpu.VMEM((heads, 8, LANES), F32),
            dma((5, heads)), dma((heads,)), dma((heads,)), dma((heads,)), dma((heads,)), dma((heads,)), dma((n,)),
            dma((heads // groups, groups * group)), dma((heads,)), dma((heads,)), dma((heads,)), dma((heads,)), dma((heads,)),
            dma((more,)), dma((more,)), dma((more,)), dma((more,)),
            dma((heads,)), dma((heads,)), dma((heads,)), dma((heads,)), dma((heads,)), dma((heads,)),
        ],
        compiler_params=pltpu.CompilerParams(
            collective_id=0, has_side_effects=True, vmem_limit_bytes=60 << 20
        ),
        name="ttt",
    )(kvq, step_sizes.T, pieces, jnp.stack([fast_gain, window_gain]))
    return pl.pallas_call(
        functools.partial(finish, heads, width, rows),
        out_shape=(
            jax.ShapeDtypeStruct(queries.shape, BF16),
            jax.ShapeDtypeStruct(fast_weights.shape, F32),
            jax.ShapeDtypeStruct(fast_weights.shape, F32),
        ),
        in_specs=[vmem] * 4,
        out_specs=(vmem, vmem, vmem),
        name="finish",
    )(out_t, grads, scales, fast_weights)


def solution(mesh):
    in_specs = (
        P(("groups", "seq"), None),
        P(("groups", "seq"), None),
        P(("groups", "seq"), None),
        P(("groups", "seq"), None),
        P("seq", None),
        P(),
        P(),
    )
    out_specs = (P(("groups", "seq"), None), P(("groups", "seq"), None), P(("groups", "seq"), None))
    return jax.shard_map(shards, mesh=mesh, in_specs=in_specs, out_specs=out_specs, check_vma=False)
```

```python
import functools
import math

import jax
import jax.numpy as jnp
from jax import lax
from jax.experimental import pallas as pl
from jax.experimental.pallas import tpu as pltpu
from jax.sharding import PartitionSpec as P

WINDOW = 1024
LANES = 128
CROSS = 4
GATHER_AT = 4
LAG = 0
F32 = jnp.float32
BF16 = jnp.bfloat16


def dot(a, b):
    return jnp.dot(a, b, preferred_element_type=F32)


def dot_nt(a, b):
    return lax.dot_general(a, b, (((1,), (1,)), ((), ())), preferred_element_type=F32)


def dot_tn(a, b):
    return lax.dot_general(a, b, (((0,), (0,)), ((), ())), preferred_element_type=F32)


def kernel(
    n, groups, heads, width,
    k_in, v_in, q_in, step_in, weights, gains,
    layer_out, new_weights, momentum,
    kvq_in, w_in, wide, out, g_out, scale_out,
    kv, qb, qx, stb, wb, wfull, wbf, kn, vt, gates, ups, hid, tgt, gg, gu,
    gstage, gother, ginc, gsend, sums, sinc, scale_send, ostage, gain_cols,
    own_o, own_l, fast_o, xo_stage, xl_stage, xo, xl,
    s_in, r_k, r_v, r_q, r_x, r_st, r_w,
    s_wf, s_x, s_xf, s_xo, s_xl, r_xo, r_xl,
    s_gp, r_gp, s_sp, r_sp, s_g, r_g, s_sc, r_sc, s_o, r_o,
):
    group = n // heads
    rows = width // n
    span = heads * LANES
    chunk = 2 * LANES
    chunks = span // chunk
    scale = 1.0 / math.sqrt(width)
    me = lax.axis_index("seq")
    part = lax.axis_index("groups")
    home_block = me // heads
    home_slot = me % heads
    near = heads - CROSS

    def place(block, which):
        odd = block % 2
        base = (block - odd) * heads
        apart = near + CROSS * odd + which
        if not near:
            return base + odd * heads + which
        j = which - CROSS
        low = j // (near // 2)
        together = 2 * j + 2 * CROSS * low + odd
        if not CROSS:
            return base + 2 * which + odd
        return base + jnp.where(which < CROSS, apart, together)

    spot = me % (2 * heads)
    pair = me // (2 * heads)
    if not CROSS:
        head = spot // 2
        member = 2 * pair + spot % 2
        paired = None
    elif near:
        low = spot < near
        high = spot >= near + 2 * CROSS
        paired = low | high
        inner = spot - near
        outer = jnp.where(low, spot, spot - 2 * CROSS)
        head = jnp.where(paired, CROSS + outer // 2, inner % CROSS)
        member = 2 * pair + jnp.where(paired, outer % 2, inner // CROSS)
    else:
        paired = None
        head = home_slot
        member = home_block
    base = member * heads
    below = member < group - 1
    above = member > 0
    stays = member == home_block

    def remote(src, dst, send, recv, device, to_part=None):
        return pltpu.make_async_remote_copy(
            src_ref=src, dst_ref=dst, send_sem=send, recv_sem=recv,
            device_id={"groups": part if to_part is None else to_part, "seq": device},
            device_id_type=pl.DeviceIdType.MESH,
        )

    barrier = pltpu.get_barrier_semaphore()
    for step in range(1, n):
        pl.semaphore_signal(
            barrier, inc=1, device_id={"seq": lax.rem(me + step, n)},
            device_id_type=pl.DeviceIdType.MESH,
        )
    for other in range(1, groups):
        for d in range(group):
            pl.semaphore_signal(
                barrier, inc=1,
                device_id={"groups": lax.rem(part + other, groups), "seq": place(d, head)},
                device_id_type=pl.DeviceIdType.MESH,
            )

    def flip(m, ref):
        for h in range(0, heads, 2):
            both = ref[:, h * width : (h + 2) * width].T
            kvq_in[h, m] = both[:width]
            kvq_in[h + 1, m] = both[width:]

    for h in range(heads):
        for m in range(3):
            at = (m * heads + h) * width
            wide[h, m * rows : (m + 1) * rows, :] = weights[:, at : at + width]
        w_in[h] = wide[h].astype(BF16)
    flip(0, k_in)
    pl.semaphore_wait(barrier, n - 1 + (groups - 1) * group)

    def landed(ref, sem):
        pltpu.make_async_copy(ref, ref, sem).wait()

    pending = []

    class Send:
        def __init__(self, src, dst, send, recv, device, local=None, only=None):
            self.ends = (src, dst, recv)
            self.copy = remote(src, dst, send, recv, device)
            self.local, self.only = local, only

        def start(self):
            if self.only is not None:
                pl.when(self.only)(self.copy.start)
            elif self.local is None:
                self.copy.start()
            else:
                pl.when(self.local)(lambda: pltpu.make_async_copy(*self.ends).start())
                pl.when(jnp.logical_not(self.local))(self.copy.start)

        def wait(self):
            if self.only is not None:
                pl.when(self.only)(self.copy.wait_send)
            elif self.local is None:
                self.copy.wait_send()
            else:
                pl.when(jnp.logical_not(self.local))(self.copy.wait_send)

    def spread(src_of, dst, recv, kind):
        sends = []
        for step in range(heads):
            which = lax.rem(head + step, heads)
            sends.append(Send(
                src_of(which), dst, s_in.at[kind, step], recv, place(home_block, which),
                stays if step == 0 else None,
            ))
        return sends

    def feed(after, sends):
        sends = list(sends)
        for done in after:
            done.wait()
            if sends:
                sends.pop(0).start()
        for send in sends:
            send.start()

    stride = heads // groups
    shift = lax.rem(part + 2 * groups * heads - home_slot - head, groups)
    w_sends = []
    for step in range(stride):
        offset = shift + groups * step
        which = lax.rem(head + offset, heads)
        w_sends.append(Send(
            w_in.at[which], wb.at[me], s_in.at[4, step], r_w.at[me], place(home_block, which),
            (offset == 0) & stays if step == 0 else None,
        ))
    feed([], w_sends)
    k_sends = spread(lambda w: kvq_in.at[w, 0], kv.at[home_slot, 0], r_k.at[home_slot], 0)
    feed([], k_sends)
    if CROSS:
        flip(2, q_in)
    x_sends = []
    for step in range(CROSS):
        which = lax.rem(head + step, CROSS)
        x_sends.append(Send(
            kvq_in.at[which, 2], qx.at[home_slot], s_x.at[step], r_x.at[home_slot],
            place(jnp.maximum(home_block - 1, 0), which), only=home_block > 0,
        ))
    feed([], x_sends)
    first = lax.rem(part + groups * heads - head, groups)

    def share_weights(slot, t, k, to_part, to_member):
        copy = remote(wb.at[slot], wb.at[slot], s_wf.at[t, k], r_w.at[slot], place(to_member, head), to_part)
        copy.start()
        pending.append(copy)

    for t in range(stride):
        slot = base + first + groups * t
        landed(wb.at[slot], r_w.at[slot])
        for d in range(1, group):
            share_weights(slot, t, d, part, lax.rem(member + d, group))
        for other in range(1, groups):
            share_weights(slot, t, other * group, lax.rem(part + other, groups), member)

    flip(1, v_in)
    v_sends = spread(lambda w: kvq_in.at[w, 1], kv.at[home_slot, 1], r_v.at[home_slot], 1)
    st_sends = spread(lambda w: step_in, stb.at[home_slot], r_st.at[home_slot], 2)
    feed(k_sends, v_sends)
    feed([], st_sends)
    if not CROSS:
        flip(2, q_in)
    q_sends = spread(lambda w: kvq_in.at[w, 2], qb.at[home_slot], r_q.at[home_slot], 3)
    for h in range(heads):
        @pl.when(head == h)
        def _():
            at = slice(h * width, (h + 1) * width)
            for m in range(2):
                row = jnp.broadcast_to(gains[m : m + 1, at], (LANES, width))
                gain_cols[m] = row.T

    for i in range(heads):
        landed(kv.at[i, 0], r_k.at[i])
        kn[i * LANES : (i + 1) * LANES, :] = kv[i, 0].T
    for d in range(1, group):
        for t in range(stride):
            slot = lax.rem(member + d, group) * heads + first + groups * t
            landed(wb.at[slot], r_w.at[slot])
            for other in range(1, groups):
                share_weights(slot, t, other * group + d, lax.rem(part + other, groups), member)
    feed(v_sends, q_sends)
    key_at = lax.broadcasted_iota(jnp.int32, (span, chunk), 0)
    lane_at = lax.broadcasted_iota(jnp.int32, (1, chunk), 1)

    def soften(scores, values):
        top = jnp.max(scores, axis=0, keepdims=True)
        powers = jnp.exp(scores - top)
        total = jnp.sum(powers, axis=0, keepdims=True)
        probs = (powers * (1.0 / total)).astype(BF16)
        return dot(values, probs), jnp.broadcast_to(top + jnp.log(total), (8, chunk))

    def normalize(field, gain):
        mean_sq = jnp.mean(field * field, axis=0, keepdims=True)
        return field * lax.rsqrt(mean_sq + 1e-05) * gain

    up_there = place(jnp.minimum(member + 1, group - 1), head)
    down_there = place(jnp.maximum(member - 1, 0), head)

    def passed(slot):
        return Send(
            qb.at[slot], qx.at[slot], s_xf.at[slot], r_x.at[slot], down_there,
            only=above if paired is None else paired & above,
        )

    def raised(slot):
        return (
            remote(xo_stage.at[slot], xo.at[slot], s_xo.at[slot], r_xo.at[slot], up_there),
            remote(xl_stage.at[slot], xl.at[slot], s_xl.at[slot], r_xl.at[slot], up_there),
        )

    def cross(c):
        start = c * chunk
        for slot in (2 * c, 2 * c + 1):
            landed(qx.at[slot], r_x.at[slot])
        query = jnp.concatenate([qx[2 * c], qx[2 * c + 1]], axis=1)
        scores = dot(kn[start:, :], query) * scale
        scores = jnp.where(key_at[start:] > lane_at + start, scores, -1e30)
        field, level = soften(scores, vt[:, start:])
        for half in range(2):
            slot = 2 * c + half
            there = slice(half * LANES, (half + 1) * LANES)
            xo_stage[slot] = field[:, there].astype(BF16)
            xl_stage[slot] = level[:, there]
            for copy in raised(slot):
                copy.start()

    def values_land():
        for i in range(heads):
            landed(kv.at[i, 1], r_v.at[i])
            there = slice(i * LANES, (i + 1) * LANES)
            vt[:, there] = kv[i, 1]

    if CROSS:
        values_land()

        @pl.when(below if paired is None else below & jnp.logical_not(paired))
        def _():
            for c in range(chunks):
                cross(c)

    for d in range(group):
        for e in range(1, groups):
            for t in range(stride):
                slot = lax.rem(member + d, group) * heads + lax.rem(first + e, groups) + groups * t
                landed(wb.at[slot], r_w.at[slot])
    for s in range(n):
        piece = wb[s].astype(F32)
        for m in range(3):
            wfull[m, s * rows : (s + 1) * rows, :] = piece[m * rows : (m + 1) * rows, :]
    for m in range(3):
        wbf[m] = wfull[m].astype(BF16)

    def gate_chunk(c, carry):
        there = pl.ds(pl.multiple_of(c * chunk, chunk), chunk)
        keys = jnp.concatenate([kv[2 * c, 0], kv[2 * c + 1, 0]], axis=1)
        gates[:, there] = dot_tn(wbf[0], keys) * scale
        ups[:, there] = dot_tn(wbf[1], keys) * scale
        return carry

    lax.fori_loop(0, chunks, gate_chunk, 0)

    if not CROSS:
        values_land()
    for i in range(heads):
        landed(stb.at[i], r_st.at[i])
        there = slice(i * LANES, (i + 1) * LANES)
        tgt[:, there] = (-stb[i, pl.ds(head, 1), :] * kv[i, 1].astype(F32)).astype(BF16)


    def grad_chunk(c, carry):
        there = pl.ds(pl.multiple_of(c * chunk, chunk), chunk)
        gate = gates[:, there]
        up = ups[:, there]
        back = dot(wbf[2], tgt[:, there]) * scale
        sigma = jax.nn.sigmoid(gate)
        silu = gate * sigma
        hid[:, there] = (silu * up).astype(BF16)
        gg[:, there] = (back * up * (sigma * (1.0 + gate * (1.0 - sigma)))).astype(BF16)
        gu[:, there] = (back * silu).astype(BF16)
        return carry

    lax.fori_loop(0, chunks, grad_chunk, 0)
    own_keys = jnp.concatenate([kv[i, 0] for i in range(heads)], axis=1)
    for m, (left, right) in enumerate(((own_keys, gg), (own_keys, gu), (hid[...], tgt))):
        grad = dot_nt(left, right[...]) * scale
        for s in range(n):
            gstage[s // heads, s % heads, m * rows : (m + 1) * rows, :] = grad[s * rows : (s + 1) * rows, :]

    for d in range(1, group):
        other = lax.rem(member + d, group)
        for i in range(heads):
            gother[d - 1, i] = gstage[other, i].astype(BF16)
        copy = remote(gother.at[d - 1], ginc.at[d - 1], s_gp.at[d - 1], r_gp.at[d - 1], place(other, head))
        copy.start()
        pending.append(copy)

    def attend(c):
        reach = (c + 1) * chunk
        query = jnp.concatenate([qb[2 * c], qb[2 * c + 1]], axis=1)
        scores = dot(kn[:reach, :], query) * scale
        scores = jnp.where(key_at[:reach] <= lane_at + c * chunk, scores, -1e30)
        attended, level = soften(scores, vt[:, :reach])
        gate = dot_tn(wbf[0], query) * scale
        up = dot_tn(wbf[1], query) * scale
        hidden = (gate * jax.nn.sigmoid(gate) * up).astype(BF16)
        fast = dot_tn(wbf[2], hidden) * scale
        for half in range(2):
            there = slice(half * LANES, (half + 1) * LANES)
            own_o[2 * c + half] = attended[:, there]
            own_l[2 * c + half] = level[:, there]
            fast_o[2 * c + half] = normalize(fast[:, there], gain_cols[0])

    def result_of(slot):
        dst = out.at[pl.ds(pl.multiple_of(head * width, 64), width), :]
        return Send(ostage.at[slot], dst, s_o.at[slot], r_o.at[head], base + slot, base + slot == me)

    def finalize(slot):
        @pl.when(above)
        def _():
            landed(xo.at[slot], r_xo.at[slot])
            landed(xl.at[slot], r_xl.at[slot])
            here = own_l[slot, 0:1, :]
            there = xl[slot, 0:1, :]
            share = 1.0 / (1.0 + jnp.exp(there - here))
            rest = 1.0 / (1.0 + jnp.exp(here - there))
            own_o[slot] = own_o[slot] * share + xo[slot].astype(F32) * rest

        ostage[slot] = (fast_o[slot] + normalize(own_o[slot], gain_cols[1])).astype(BF16)
        result_of(slot).start()

    def g_sends(src_of, dst, send, recv):
        sends = []
        for step in range(heads):
            i = lax.rem(home_slot + step, heads)
            sends.append(Send(src_of(i), dst.at[head], send.at[step], recv.at[head], base + i, stays if step == 0 else None))
        return sends

    def partner_sums():
        return [
            remote(sums, sinc.at[d - 1], s_sp.at[d - 1], r_sp.at[d - 1], place(lax.rem(member + d, group), head))
            for d in range(1, group)
        ]

    def gather_gradient():
        for d in range(1, group):
            landed(ginc.at[d - 1], r_gp.at[d - 1])
        sums[...] = jnp.zeros_like(sums)

        def add_up(i, carry):
            total = gstage[member, i]
            for d in range(1, group):
                total = total + ginc[d - 1, i].astype(F32)
            gsend[i] = total.astype(BF16)
            weight = wb[base + i].astype(F32)
            moved = weight - total
            for m in range(3):
                piece = slice(m * rows, (m + 1) * rows)
                old = weight[piece, :]
                new = moved[piece, :]
                sums[m : m + 1, :] += jnp.sum(old * old, axis=0, keepdims=True)
                sums[4 + m : 5 + m, :] += jnp.sum(new * new, axis=0, keepdims=True)
            return carry

        lax.fori_loop(0, heads, add_up, 0)
        for copy in partner_sums():
            copy.start()
        for send in g_sends(lambda i: gsend.at[i], g_out, s_g, r_g):
            send.start()

    def send_scales():
        for d in range(1, group):
            landed(sinc.at[d - 1], r_sp.at[d - 1])
        total = sums[...]
        for d in range(1, group):
            total = total + sinc[d - 1]
        scale_send[0:4, :] = jnp.sqrt((total[0:4] + 1e-06) / (total[4:8] + 1e-06))
        scale_send[4:8, :] = total[4:8]
        for send in g_sends(lambda i: scale_send, scale_out, s_sc, r_sc):
            send.start()

    turn = head % chunks
    if near:
        for t in range(heads):
            slot = lax.rem(2 * turn + t, heads)
            landed(qb.at[slot], r_q.at[slot])
            passed(slot).start()
    else:
        for slot in range(heads):
            landed(qb.at[slot], r_q.at[slot])

    def work(t, carry):
        now = lax.rem(turn + t, chunks)
        for c in range(chunks):
            @pl.when(now == c)
            def _():
                if near:
                    pl.when(below if paired is None else below & paired)(lambda: cross(c))
                attend(c)

        if GATHER_AT < chunks:
            pl.when(t == GATHER_AT)(gather_gradient)
            pl.when(t == GATHER_AT + 1)(send_scales)
        if LAG:
            @pl.when(t > 0)
            def _():
                before = lax.rem(turn + t + chunks - 1, chunks)
                finalize(2 * before)
                finalize(2 * before + 1)
        else:
            finalize(2 * now)
            finalize(2 * now + 1)
        return carry

    lax.fori_loop(0, chunks, work, 0)
    if GATHER_AT >= chunks:
        gather_gradient()
        send_scales()
    if LAG:
        last = lax.rem(turn + chunks - 1, chunks)
        finalize(2 * last)
        finalize(2 * last + 1)

    for h in range(heads):
        landed(g_out.at[h], r_g.at[h])
        landed(scale_out.at[h], r_sc.at[h])
        grad = g_out[h].astype(F32)
        for m in range(3):
            at = (m * heads + h) * width
            piece = grad[m * rows : (m + 1) * rows, :]
            momentum[:, at : at + width] = piece
            new_weights[:, at : at + width] = (weights[:, at : at + width] - piece) * scale_out[h, m : m + 1, :]

    for copy in pending:
        copy.wait_send()
    for send in w_sends + st_sends + x_sends + q_sends:
        send.wait()
    for send in g_sends(lambda i: gsend.at[i], g_out, s_g, r_g) + g_sends(lambda i: scale_send, scale_out, s_sc, r_sc):
        send.wait()
    for copy in partner_sums():
        copy.wait_send()
    if near:
        for slot in range(heads):
            passed(slot).wait()

    @pl.when(below)
    def _():
        for slot in range(heads):
            for copy in raised(slot):
                copy.wait_send()

    for h in range(0, heads, 2):
        for i in (h, h + 1):
            landed(out.at[pl.ds(i * width, width), :], r_o.at[i])
        layer_out[:, h * width : (h + 2) * width] = out[h * width : (h + 2) * width, :].T
    for slot in range(heads):
        result_of(slot).wait()


def hand_over(a, b, c, x, y, z):
    x[...] = a[...]
    y[...] = b[...]
    z[...] = c[...]


def shards(queries, key_vectors, value_vectors, step_sizes, fast_weights, fast_gain, window_gain):
    tokens = queries.shape[0]
    heads = step_sizes.shape[1]
    width = queries.shape[1] // heads
    n = lax.axis_size("seq")
    groups = lax.axis_size("groups")
    group = n // heads
    rows = width // n
    assert tokens == LANES and heads * tokens == WINDOW and group % 2 == 0
    span = heads * LANES
    vmem = pl.BlockSpec(memory_space=pltpu.VMEM)
    dma = pltpu.SemaphoreType.DMA
    more = max(group - 1, 1)
    token_piece = pltpu.VMEM((heads, width, LANES), BF16)
    level_piece = pltpu.VMEM((heads, 8, LANES), F32)
    weight_piece = pltpu.VMEM((heads, 3 * rows, width), BF16)
    across = pltpu.VMEM((width, span), BF16)
    across_wide = pltpu.VMEM((width, span), F32)
    results = pl.pallas_call(
        functools.partial(kernel, n, groups, heads, width),
        out_shape=(
            jax.ShapeDtypeStruct(queries.shape, BF16),
            jax.ShapeDtypeStruct(fast_weights.shape, F32),
            jax.ShapeDtypeStruct(fast_weights.shape, F32),
        ),
        in_specs=[vmem] * 6,
        out_specs=(vmem, vmem, vmem),
        scratch_shapes=[
            pltpu.VMEM((heads, 3, width, LANES), BF16),
            weight_piece,
            pltpu.VMEM((heads, 3 * rows, width), F32),
            pltpu.VMEM((heads * width, LANES), BF16),
            weight_piece,
            pltpu.VMEM((heads, 8, width), F32),
            pltpu.VMEM((heads, 2, width, LANES), BF16),
            token_piece,
            token_piece,
            pltpu.VMEM((heads, heads, LANES), F32),
            pltpu.VMEM((n, 3 * rows, width), BF16),
            pltpu.VMEM((3, width, width), F32),
            pltpu.VMEM((3, width, width), BF16),
            pltpu.VMEM((span, width), BF16),
            across,
            across_wide, across_wide, across, across, across, across,
            pltpu.VMEM((group, heads, 3 * rows, width), F32),
            pltpu.VMEM((more, heads, 3 * rows, width), BF16),
            pltpu.VMEM((more, heads, 3 * rows, width), BF16),
            weight_piece,
            pltpu.VMEM((8, width), F32),
            pltpu.VMEM((more, 8, width), F32),
            pltpu.VMEM((8, width), F32),
            token_piece,
            pltpu.VMEM((2, width, LANES), F32),
            pltpu.VMEM((heads, width, LANES), F32),
            level_piece,
            pltpu.VMEM((heads, width, LANES), F32),
            token_piece,
            level_piece,
            token_piece,
            level_piece,
            dma((5, heads)), dma((heads,)), dma((heads,)), dma((heads,)), dma((heads,)), dma((heads,)), dma((n,)),
            dma((heads // groups, groups * group)), dma((heads,)), dma((heads,)),
            dma((heads,)), dma((heads,)), dma((heads,)), dma((heads,)),
            dma((more,)), dma((more,)), dma((more,)), dma((more,)),
            dma((heads,)), dma((heads,)), dma((heads,)), dma((heads,)), dma((heads,)), dma((heads,)),
        ],
        compiler_params=pltpu.CompilerParams(
            collective_id=0, has_side_effects=True, vmem_limit_bytes=60 << 20
        ),
        name="ttt",
    )(key_vectors, value_vectors, queries, step_sizes.T, fast_weights, jnp.stack([fast_gain, window_gain]))
    return pl.pallas_call(
        hand_over,
        out_shape=tuple(jax.ShapeDtypeStruct(r.shape, r.dtype) for r in results),
        in_specs=[vmem] * 3,
        out_specs=(vmem,) * 3,
        name="hand_over",
    )(*results)


def solution(mesh):
    in_specs = (
        P(("groups", "seq"), None),
        P(("groups", "seq"), None),
        P(("groups", "seq"), None),
        P(("groups", "seq"), None),
        P("seq", None),
        P(),
        P(),
    )
    out_specs = (P(("groups", "seq"), None), P(("groups", "seq"), None), P(("groups", "seq"), None))
    return jax.shard_map(shards, mesh=mesh, in_specs=in_specs, out_specs=out_specs, check_vma=False)
```

```python
import functools
import math

import jax
import jax.numpy as jnp
from jax import lax
from jax.experimental import pallas as pl
from jax.experimental.pallas import tpu as pltpu
from jax.sharding import PartitionSpec as P

WINDOW = 1024
LANES = 128
CROSS = 0
GATHER_AT = 1
LAG = 0
F32 = jnp.float32
BF16 = jnp.bfloat16


def dot(a, b):
    return jnp.dot(a, b, preferred_element_type=F32)


def dot_nt(a, b):
    return lax.dot_general(a, b, (((1,), (1,)), ((), ())), preferred_element_type=F32)


def dot_tn(a, b):
    return lax.dot_general(a, b, (((0,), (0,)), ((), ())), preferred_element_type=F32)


def kernel(
    n, groups, heads, width,
    k_in, v_in, q_in, step_in, weights, fast_gain, window_gain,
    out, g_out, scale_out,
    kvq_in, w_in, wide,
    kv, qb, qx, stb, wb, wfull, wbf, kn, vt, gates, ups, hid, tgt, gg, gu,
    gstage, gother, ginc, gsend, sums, sinc, scale_send, ostage, gain_cols,
    own_o, own_l, fast_o, xo_stage, xl_stage, xo, xl,
    s_in, r_k, r_v, r_q, r_x, r_st, r_w,
    s_wf, s_x, s_xf, s_xo, s_xl, r_xo, r_xl,
    s_gp, r_gp, s_sp, r_sp, s_g, r_g, s_sc, r_sc, s_o, r_o,
):
    group = n // heads
    rows = width // n
    span = heads * LANES
    chunk = 2 * LANES
    chunks = span // chunk
    scale = 1.0 / math.sqrt(width)
    me = lax.axis_index("seq")
    part = lax.axis_index("groups")
    home_block = me // heads
    home_slot = me % heads
    near = heads - CROSS

    def place(block, which):
        odd = block % 2
        base = (block - odd) * heads
        apart = near + CROSS * odd + which
        if not near:
            return base + odd * heads + which
        j = which - CROSS
        low = j // (near // 2)
        together = 2 * j + 2 * CROSS * low + odd
        if not CROSS:
            return base + 2 * which + odd
        return base + jnp.where(which < CROSS, apart, together)

    spot = me % (2 * heads)
    pair = me // (2 * heads)
    if not CROSS:
        head = spot // 2
        member = 2 * pair + spot % 2
        paired = None
    elif near:
        low = spot < near
        high = spot >= near + 2 * CROSS
        paired = low | high
        inner = spot - near
        outer = jnp.where(low, spot, spot - 2 * CROSS)
        head = jnp.where(paired, CROSS + outer // 2, inner % CROSS)
        member = 2 * pair + jnp.where(paired, outer % 2, inner // CROSS)
    else:
        paired = None
        head = home_slot
        member = home_block
    base = member * heads
    below = member < group - 1
    above = member > 0
    stays = member == home_block

    def remote(src, dst, send, recv, device, to_part=None):
        return pltpu.make_async_remote_copy(
            src_ref=src, dst_ref=dst, send_sem=send, recv_sem=recv,
            device_id={"groups": part if to_part is None else to_part, "seq": device},
            device_id_type=pl.DeviceIdType.MESH,
        )

    barrier = pltpu.get_barrier_semaphore()
    for step in range(1, n):
        pl.semaphore_signal(
            barrier, inc=1, device_id={"seq": lax.rem(me + step, n)},
            device_id_type=pl.DeviceIdType.MESH,
        )
    for other in range(1, groups):
        for d in range(group):
            pl.semaphore_signal(
                barrier, inc=1,
                device_id={"groups": lax.rem(part + other, groups), "seq": place(d, head)},
                device_id_type=pl.DeviceIdType.MESH,
            )

    def flip(m, ref):
        for h in range(0, heads, 2):
            both = ref[:, h * width : (h + 2) * width].T
            kvq_in[h, m] = both[:width]
            kvq_in[h + 1, m] = both[width:]

    for h in range(heads):
        for m in range(3):
            at = (m * heads + h) * width
            wide[h, m * rows : (m + 1) * rows, :] = weights[:, at : at + width]
        w_in[h] = wide[h].astype(BF16)
    flip(0, k_in)
    pl.semaphore_wait(barrier, n - 1 + (groups - 1) * group)

    def landed(ref, sem):
        pltpu.make_async_copy(ref, ref, sem).wait()

    pending = []

    class Send:
        def __init__(self, src, dst, send, recv, device, local=None, only=None):
            self.ends = (src, dst, recv)
            self.copy = remote(src, dst, send, recv, device)
            self.local, self.only = local, only

        def start(self):
            if self.only is not None:
                pl.when(self.only)(self.copy.start)
            elif self.local is None:
                self.copy.start()
            else:
                pl.when(self.local)(lambda: pltpu.make_async_copy(*self.ends).start())
                pl.when(jnp.logical_not(self.local))(self.copy.start)

        def wait(self):
            if self.only is not None:
                pl.when(self.only)(self.copy.wait_send)
            elif self.local is None:
                self.copy.wait_send()
            else:
                pl.when(jnp.logical_not(self.local))(self.copy.wait_send)

    def spread(src_of, dst, recv, kind):
        sends = []
        for step in range(heads):
            which = lax.rem(head + step, heads)
            sends.append(Send(
                src_of(which), dst, s_in.at[kind, step], recv, place(home_block, which),
                stays if step == 0 else None,
            ))
        return sends

    def feed(after, sends):
        sends = list(sends)
        for done in after:
            done.wait()
            if sends:
                sends.pop(0).start()
        for send in sends:
            send.start()

    stride = heads // groups
    shift = lax.rem(part + 2 * groups * heads - home_slot - head, groups)
    w_sends = []
    for step in range(stride):
        offset = shift + groups * step
        which = lax.rem(head + offset, heads)
        w_sends.append(Send(
            w_in.at[which], wb.at[me], s_in.at[4, step], r_w.at[me], place(home_block, which),
            (offset == 0) & stays if step == 0 else None,
        ))
    feed([], w_sends)
    k_sends = spread(lambda w: kvq_in.at[w, 0], kv.at[home_slot, 0], r_k.at[home_slot], 0)
    feed([], k_sends)
    if CROSS:
        flip(2, q_in)
    x_sends = []
    for step in range(CROSS):
        which = lax.rem(head + step, CROSS)
        x_sends.append(Send(
            kvq_in.at[which, 2], qx.at[home_slot], s_x.at[step], r_x.at[home_slot],
            place(jnp.maximum(home_block - 1, 0), which), only=home_block > 0,
        ))
    feed([], x_sends)
    first = lax.rem(part + groups * heads - head, groups)

    def share_weights(slot, t, k, to_part, to_member):
        copy = remote(wb.at[slot], wb.at[slot], s_wf.at[t, k], r_w.at[slot], place(to_member, head), to_part)
        copy.start()
        pending.append(copy)

    for t in range(stride):
        slot = base + first + groups * t
        landed(wb.at[slot], r_w.at[slot])
        for d in range(1, group):
            share_weights(slot, t, d, part, lax.rem(member + d, group))
        for other in range(1, groups):
            share_weights(slot, t, other * group, lax.rem(part + other, groups), member)

    flip(1, v_in)
    v_sends = spread(lambda w: kvq_in.at[w, 1], kv.at[home_slot, 1], r_v.at[home_slot], 1)
    st_sends = spread(lambda w: step_in, stb.at[home_slot], r_st.at[home_slot], 2)
    feed(k_sends, v_sends)
    feed([], st_sends)
    if not CROSS:
        flip(2, q_in)
    q_sends = spread(lambda w: kvq_in.at[w, 2], qb.at[home_slot], r_q.at[home_slot], 3)
    for h in range(heads):
        @pl.when(head == h)
        def _():
            at = slice(h * width, (h + 1) * width)
            for m, gain in enumerate((fast_gain, window_gain)):
                gain_cols[m] = jnp.broadcast_to(gain[at].reshape(1, width), (LANES, width)).T

    for i in range(heads):
        landed(kv.at[i, 0], r_k.at[i])
        kn[i * LANES : (i + 1) * LANES, :] = kv[i, 0].T
    for d in range(1, group):
        for t in range(stride):
            slot = lax.rem(member + d, group) * heads + first + groups * t
            landed(wb.at[slot], r_w.at[slot])
            for other in range(1, groups):
                share_weights(slot, t, other * group + d, lax.rem(part + other, groups), member)
    feed(v_sends, q_sends)
    key_at = lax.broadcasted_iota(jnp.int32, (span, chunk), 0)
    lane_at = lax.broadcasted_iota(jnp.int32, (1, chunk), 1)

    def soften(scores, values):
        top = jnp.max(scores, axis=0, keepdims=True)
        powers = jnp.exp(scores - top)
        total = jnp.sum(powers, axis=0, keepdims=True)
        probs = (powers * (1.0 / total)).astype(BF16)
        return dot(values, probs), jnp.broadcast_to(top + jnp.log(total), (8, chunk))

    def normalize(field, gain):
        mean_sq = jnp.mean(field * field, axis=0, keepdims=True)
        return field * lax.rsqrt(mean_sq + 1e-05) * gain

    up_there = place(jnp.minimum(member + 1, group - 1), head)
    down_there = place(jnp.maximum(member - 1, 0), head)

    def passed(slot):
        return Send(
            qb.at[slot], qx.at[slot], s_xf.at[slot], r_x.at[slot], down_there,
            only=above if paired is None else paired & above,
        )

    def raised(slot):
        return (
            remote(xo_stage.at[slot], xo.at[slot], s_xo.at[slot], r_xo.at[slot], up_there),
            remote(xl_stage.at[slot], xl.at[slot], s_xl.at[slot], r_xl.at[slot], up_there),
        )

    def cross(c):
        start = c * chunk
        for slot in (2 * c, 2 * c + 1):
            landed(qx.at[slot], r_x.at[slot])
        query = jnp.concatenate([qx[2 * c], qx[2 * c + 1]], axis=1)
        scores = dot(kn[start:, :], query) * scale
        scores = jnp.where(key_at[start:] > lane_at + start, scores, -1e30)
        field, level = soften(scores, vt[:, start:])
        for half in range(2):
            slot = 2 * c + half
            there = slice(half * LANES, (half + 1) * LANES)
            xo_stage[slot] = field[:, there].astype(BF16)
            xl_stage[slot] = level[:, there]
            for copy in raised(slot):
                copy.start()

    def values_land():
        for i in range(heads):
            landed(kv.at[i, 1], r_v.at[i])
            there = slice(i * LANES, (i + 1) * LANES)
            vt[:, there] = kv[i, 1]

    if CROSS:
        values_land()

        @pl.when(below if paired is None else below & jnp.logical_not(paired))
        def _():
            for c in range(chunks):
                cross(c)

    for d in range(group):
        for e in range(1, groups):
            for t in range(stride):
                slot = lax.rem(member + d, group) * heads + lax.rem(first + e, groups) + groups * t
                landed(wb.at[slot], r_w.at[slot])
    for s in range(n):
        piece = wb[s].astype(F32)
        for m in range(3):
            wfull[m, s * rows : (s + 1) * rows, :] = piece[m * rows : (m + 1) * rows, :]
    for m in range(3):
        wbf[m] = wfull[m].astype(BF16)

    def gate_chunk(c, carry):
        there = pl.ds(pl.multiple_of(c * chunk, chunk), chunk)
        keys = jnp.concatenate([kv[2 * c, 0], kv[2 * c + 1, 0]], axis=1)
        gates[:, there] = dot_tn(wbf[0], keys) * scale
        ups[:, there] = dot_tn(wbf[1], keys) * scale
        return carry

    lax.fori_loop(0, chunks, gate_chunk, 0)

    if not CROSS:
        values_land()
    for i in range(heads):
        landed(stb.at[i], r_st.at[i])
        there = slice(i * LANES, (i + 1) * LANES)
        tgt[:, there] = (-stb[i, pl.ds(head, 1), :] * kv[i, 1].astype(F32)).astype(BF16)


    def grad_chunk(c, carry):
        there = pl.ds(pl.multiple_of(c * chunk, chunk), chunk)
        gate = gates[:, there]
        up = ups[:, there]
        back = dot(wbf[2], tgt[:, there]) * scale
        sigma = jax.nn.sigmoid(gate)
        silu = gate * sigma
        hid[:, there] = (silu * up).astype(BF16)
        gg[:, there] = (back * up * (sigma * (1.0 + gate * (1.0 - sigma)))).astype(BF16)
        gu[:, there] = (back * silu).astype(BF16)
        return carry

    lax.fori_loop(0, chunks, grad_chunk, 0)
    own_keys = jnp.concatenate([kv[i, 0] for i in range(heads)], axis=1)
    for m, (left, right) in enumerate(((own_keys, gg), (own_keys, gu), (hid[...], tgt))):
        grad = dot_nt(left, right[...]) * scale
        for s in range(n):
            gstage[s // heads, s % heads, m * rows : (m + 1) * rows, :] = grad[s * rows : (s + 1) * rows, :]

    for d in range(1, group):
        other = lax.rem(member + d, group)
        for i in range(heads):
            gother[d - 1, i] = gstage[other, i].astype(BF16)
        copy = remote(gother.at[d - 1], ginc.at[d - 1], s_gp.at[d - 1], r_gp.at[d - 1], place(other, head))
        copy.start()
        pending.append(copy)

    def attend(c):
        reach = (c + 1) * chunk
        query = jnp.concatenate([qb[2 * c], qb[2 * c + 1]], axis=1)
        scores = dot(kn[:reach, :], query) * scale
        scores = jnp.where(key_at[:reach] <= lane_at + c * chunk, scores, -1e30)
        attended, level = soften(scores, vt[:, :reach])
        gate = dot_tn(wbf[0], query) * scale
        up = dot_tn(wbf[1], query) * scale
        hidden = (gate * jax.nn.sigmoid(gate) * up).astype(BF16)
        fast = dot_tn(wbf[2], hidden) * scale
        for half in range(2):
            there = slice(half * LANES, (half + 1) * LANES)
            own_o[2 * c + half] = attended[:, there]
            own_l[2 * c + half] = level[:, there]
            fast_o[2 * c + half] = normalize(fast[:, there], gain_cols[0])

    def result_of(slot):
        dst = out.at[pl.ds(pl.multiple_of(head * width, 64), width), :]
        return Send(ostage.at[slot], dst, s_o.at[slot], r_o.at[head], base + slot, base + slot == me)

    def finalize(slot):
        @pl.when(above)
        def _():
            landed(xo.at[slot], r_xo.at[slot])
            landed(xl.at[slot], r_xl.at[slot])
            here = own_l[slot, 0:1, :]
            there = xl[slot, 0:1, :]
            share = 1.0 / (1.0 + jnp.exp(there - here))
            rest = 1.0 / (1.0 + jnp.exp(here - there))
            own_o[slot] = own_o[slot] * share + xo[slot].astype(F32) * rest

        ostage[slot] = (fast_o[slot] + normalize(own_o[slot], gain_cols[1])).astype(BF16)
        result_of(slot).start()

    def g_sends(src_of, dst, send, recv):
        sends = []
        for step in range(heads):
            i = lax.rem(home_slot + step, heads)
            sends.append(Send(src_of(i), dst.at[head], send.at[step], recv.at[head], base + i, stays if step == 0 else None))
        return sends

    def partner_sums():
        return [
            remote(sums, sinc.at[d - 1], s_sp.at[d - 1], r_sp.at[d - 1], place(lax.rem(member + d, group), head))
            for d in range(1, group)
        ]

    def gather_gradient():
        for d in range(1, group):
            landed(ginc.at[d - 1], r_gp.at[d - 1])
        sums[...] = jnp.zeros_like(sums)

        def add_up(i, carry):
            total = gstage[member, i]
            for d in range(1, group):
                total = total + ginc[d - 1, i].astype(F32)
            gsend[i] = total.astype(BF16)
            weight = wb[base + i].astype(F32)
            moved = weight - total
            for m in range(3):
                piece = slice(m * rows, (m + 1) * rows)
                old = weight[piece, :]
                new = moved[piece, :]
                sums[m : m + 1, :] += jnp.sum(old * old, axis=0, keepdims=True)
                sums[4 + m : 5 + m, :] += jnp.sum(new * new, axis=0, keepdims=True)
            return carry

        lax.fori_loop(0, heads, add_up, 0)
        for copy in partner_sums():
            copy.start()
        for send in g_sends(lambda i: gsend.at[i], g_out, s_g, r_g):
            send.start()

    def send_scales():
        for d in range(1, group):
            landed(sinc.at[d - 1], r_sp.at[d - 1])
        total = sums[...]
        for d in range(1, group):
            total = total + sinc[d - 1]
        scale_send[0:4, :] = jnp.sqrt((total[0:4] + 1e-06) / (total[4:8] + 1e-06))
        scale_send[4:8, :] = total[4:8]
        for send in g_sends(lambda i: scale_send, scale_out, s_sc, r_sc):
            send.start()

    late = member >= 0
    if near:
        if CROSS:
            late = jnp.logical_not(paired)
            early = paired
        else:
            early = member >= 0
            late = member < 0

        @pl.when(early)
        def _():
            gather_gradient()
            send_scales()

    turn = head % chunks
    if near:
        for t in range(heads):
            slot = lax.rem(2 * turn + t, heads)
            landed(qb.at[slot], r_q.at[slot])
            passed(slot).start()
    else:
        for slot in range(heads):
            landed(qb.at[slot], r_q.at[slot])

    def work(t, carry):
        now = lax.rem(turn + t, chunks)
        for c in range(chunks):
            @pl.when(now == c)
            def _():
                if near:
                    pl.when(below if paired is None else below & paired)(lambda: cross(c))
                attend(c)

        if GATHER_AT < chunks:
            pl.when(late & (t == GATHER_AT))(gather_gradient)
        if GATHER_AT + 1 < chunks:
            pl.when(late & (t == GATHER_AT + 1))(send_scales)
        if LAG:
            @pl.when(t > 0)
            def _():
                before = lax.rem(turn + t + chunks - 1, chunks)
                finalize(2 * before)
                finalize(2 * before + 1)
        else:
            finalize(2 * now)
            finalize(2 * now + 1)
        return carry

    lax.fori_loop(0, chunks, work, 0)
    if GATHER_AT + 1 >= chunks:
        @pl.when(late)
        def _():
            if GATHER_AT >= chunks:
                gather_gradient()
            send_scales()
    if LAG:
        last = lax.rem(turn + chunks - 1, chunks)
        finalize(2 * last)
        finalize(2 * last + 1)

    for copy in pending:
        copy.wait_send()
    for send in w_sends + st_sends + x_sends + q_sends:
        send.wait()
    for send in g_sends(lambda i: gsend.at[i], g_out, s_g, r_g) + g_sends(lambda i: scale_send, scale_out, s_sc, r_sc):
        send.wait()
    for copy in partner_sums():
        copy.wait_send()
    if near:
        for slot in range(heads):
            passed(slot).wait()

    @pl.when(below)
    def _():
        for slot in range(heads):
            for copy in raised(slot):
                copy.wait_send()

    for h in range(heads):
        landed(g_out.at[h], r_g.at[h])
        landed(scale_out.at[h], r_sc.at[h])
        landed(out.at[pl.ds(h * width, width), :], r_o.at[h])
    for slot in range(heads):
        result_of(slot).wait()


def finish(heads, width, rows, out_t, grads, scales, weights, layer_out, new_weights, momentum):
    layer_out[...] = out_t[...].T
    for h in range(heads):
        grad = grads[h].astype(F32)
        for m in range(3):
            at = (m * heads + h) * width
            part = grad[m * rows : (m + 1) * rows, :]
            momentum[:, at : at + width] = part
            new_weights[:, at : at + width] = (weights[:, at : at + width] - part) * scales[h, m : m + 1, :]


def shards(queries, key_vectors, value_vectors, step_sizes, fast_weights, fast_gain, window_gain):
    tokens = queries.shape[0]
    heads = step_sizes.shape[1]
    width = queries.shape[1] // heads
    n = lax.axis_size("seq")
    groups = lax.axis_size("groups")
    group = n // heads
    rows = width // n
    assert tokens == LANES and heads * tokens == WINDOW and group % 2 == 0
    span = heads * LANES
    vmem = pl.BlockSpec(memory_space=pltpu.VMEM)
    dma = pltpu.SemaphoreType.DMA
    more = max(group - 1, 1)
    token_piece = pltpu.VMEM((heads, width, LANES), BF16)
    level_piece = pltpu.VMEM((heads, 8, LANES), F32)
    weight_piece = pltpu.VMEM((heads, 3 * rows, width), BF16)
    across = pltpu.VMEM((width, span), BF16)
    across_wide = pltpu.VMEM((width, span), F32)
    out_t, grads, scales = pl.pallas_call(
        functools.partial(kernel, n, groups, heads, width),
        out_shape=(
            jax.ShapeDtypeStruct((heads * width, LANES), BF16),
            jax.ShapeDtypeStruct((heads, 3 * rows, width), BF16),
            jax.ShapeDtypeStruct((heads, 8, width), F32),
        ),
        in_specs=[vmem] * 7,
        out_specs=(vmem, vmem, vmem),
        scratch_shapes=[
            pltpu.VMEM((heads, 3, width, LANES), BF16),
            weight_piece,
            pltpu.VMEM((heads, 3 * rows, width), F32),
            pltpu.VMEM((heads, 2, width, LANES), BF16),
            token_piece,
            token_piece,
            pltpu.VMEM((heads, heads, LANES), F32),
            pltpu.VMEM((n, 3 * rows, width), BF16),
            pltpu.VMEM((3, width, width), F32),
            pltpu.VMEM((3, width, width), BF16),
            pltpu.VMEM((span, width), BF16),
            across,
            across_wide, across_wide, across, across, across, across,
            pltpu.VMEM((group, heads, 3 * rows, width), F32),
            pltpu.VMEM((more, heads, 3 * rows, width), BF16),
            pltpu.VMEM((more, heads, 3 * rows, width), BF16),
            weight_piece,
            pltpu.VMEM((8, width), F32),
            pltpu.VMEM((more, 8, width), F32),
            pltpu.VMEM((8, width), F32),
            token_piece,
            pltpu.VMEM((2, width, LANES), F32),
            pltpu.VMEM((heads, width, LANES), F32),
            level_piece,
            pltpu.VMEM((heads, width, LANES), F32),
            token_piece,
            level_piece,
            token_piece,
            level_piece,
            dma((5, heads)), dma((heads,)), dma((heads,)), dma((heads,)), dma((heads,)), dma((heads,)), dma((n,)),
            dma((heads // groups, groups * group)), dma((heads,)), dma((heads,)),
            dma((heads,)), dma((heads,)), dma((heads,)), dma((heads,)),
            dma((more,)), dma((more,)), dma((more,)), dma((more,)),
            dma((heads,)), dma((heads,)), dma((heads,)), dma((heads,)), dma((heads,)), dma((heads,)),
        ],
        compiler_params=pltpu.CompilerParams(
            collective_id=0, has_side_effects=True, vmem_limit_bytes=60 << 20
        ),
        name="ttt",
    )(key_vectors, value_vectors, queries, step_sizes.T, fast_weights, fast_gain, window_gain)
    return pl.pallas_call(
        functools.partial(finish, heads, width, rows),
        out_shape=(
            jax.ShapeDtypeStruct(queries.shape, BF16),
            jax.ShapeDtypeStruct(fast_weights.shape, F32),
            jax.ShapeDtypeStruct(fast_weights.shape, F32),
        ),
        in_specs=[vmem] * 4,
        out_specs=(vmem, vmem, vmem),
        name="finish",
    )(out_t, grads, scales, fast_weights)


def solution(mesh):
    in_specs = (
        P(("groups", "seq"), None),
        P(("groups", "seq"), None),
        P(("groups", "seq"), None),
        P(("groups", "seq"), None),
        P("seq", None),
        P(),
        P(),
    )
    out_specs = (P(("groups", "seq"), None), P(("groups", "seq"), None), P(("groups", "seq"), None))
    return jax.shard_map(shards, mesh=mesh, in_specs=in_specs, out_specs=out_specs, check_vma=False)
```

```python
import functools
import math

import jax
import jax.numpy as jnp
from jax import lax
from jax.experimental import pallas as pl
from jax.experimental.pallas import tpu as pltpu
from jax.sharding import PartitionSpec as P

WINDOW = 1024
LANES = 128
CROSS = 0
GATHER_AT = 1
LAG = 0
G_LATE = 0
GATE = 0
F32 = jnp.float32
BF16 = jnp.bfloat16


def dot(a, b):
    return jnp.dot(a, b, preferred_element_type=F32)


def dot_nt(a, b):
    return lax.dot_general(a, b, (((1,), (1,)), ((), ())), preferred_element_type=F32)


def dot_tn(a, b):
    return lax.dot_general(a, b, (((0,), (0,)), ((), ())), preferred_element_type=F32)


def kernel(
    n, groups, heads, width,
    k_hbm, v_hbm, q_hbm, step_in, w_hbm, fast_gain, window_gain,
    out, g_out, scale_out,
    k_in, v_in, q_in, weights, s_load,
    kvq_in, w_in, wide,
    kv, qb, qx, stb, wb, wfull, wbf, kn, vt, gates, ups, hid, tgt, gg, gu,
    gstage, gother, ginc, gsend, sums, sinc, scale_send, ostage, gain_cols,
    own_o, own_l, fast_o, xo_stage, xl_stage, xo, xl,
    s_in, r_k, r_v, r_q, r_x, r_st, r_w,
    s_wf, s_x, s_xf, s_xo, s_xl, r_xo, r_xl,
    s_gp, r_gp, s_sp, r_sp, s_g, r_g, s_sc, r_sc, s_o, r_o,
):
    group = n // heads
    rows = width // n
    span = heads * LANES
    chunk = 2 * LANES
    chunks = span // chunk
    scale = 1.0 / math.sqrt(width)
    me = lax.axis_index("seq")
    part = lax.axis_index("groups")
    home_block = me // heads
    home_slot = me % heads
    near = heads - CROSS

    def place(block, which):
        odd = block % 2
        base = (block - odd) * heads
        apart = near + CROSS * odd + which
        if not near:
            return base + odd * heads + which
        j = which - CROSS
        low = j // (near // 2)
        together = 2 * j + 2 * CROSS * low + odd
        if not CROSS:
            return base + 2 * which + odd
        return base + jnp.where(which < CROSS, apart, together)

    spot = me % (2 * heads)
    pair = me // (2 * heads)
    if not CROSS:
        head = spot // 2
        member = 2 * pair + spot % 2
        paired = None
    elif near:
        low = spot < near
        high = spot >= near + 2 * CROSS
        paired = low | high
        inner = spot - near
        outer = jnp.where(low, spot, spot - 2 * CROSS)
        head = jnp.where(paired, CROSS + outer // 2, inner % CROSS)
        member = 2 * pair + jnp.where(paired, outer % 2, inner // CROSS)
    else:
        paired = None
        head = home_slot
        member = home_block
    base = member * heads
    below = member < group - 1
    above = member > 0
    stays = member == home_block

    def remote(src, dst, send, recv, device, to_part=None):
        return pltpu.make_async_remote_copy(
            src_ref=src, dst_ref=dst, send_sem=send, recv_sem=recv,
            device_id={"groups": part if to_part is None else to_part, "seq": device},
            device_id_type=pl.DeviceIdType.MESH,
        )

    loads = [
        pltpu.make_async_copy(src, dst, s_load.at[i])
        for i, (src, dst) in enumerate(((w_hbm, weights), (k_hbm, k_in), (v_hbm, v_in), (q_hbm, q_in)))
    ]
    for load in loads:
        load.start()
    barrier = pltpu.get_barrier_semaphore()
    for step in range(1, n):
        pl.semaphore_signal(
            barrier, inc=1, device_id={"seq": lax.rem(me + step, n)},
            device_id_type=pl.DeviceIdType.MESH,
        )
    for other in range(1, groups):
        for d in range(group):
            pl.semaphore_signal(
                barrier, inc=1,
                device_id={"groups": lax.rem(part + other, groups), "seq": place(d, head)},
                device_id_type=pl.DeviceIdType.MESH,
            )

    def flip(m, ref):
        for h in range(0, heads, 2):
            both = ref[:, h * width : (h + 2) * width].T
            kvq_in[h, m] = both[:width]
            kvq_in[h + 1, m] = both[width:]

    loads[0].wait()
    for h in range(heads):
        for m in range(3):
            at = (m * heads + h) * width
            wide[h, m * rows : (m + 1) * rows, :] = weights[:, at : at + width]
        w_in[h] = wide[h].astype(BF16)
    loads[1].wait()
    flip(0, k_in)
    pl.semaphore_wait(barrier, n - 1 + (groups - 1) * group)

    def landed(ref, sem):
        pltpu.make_async_copy(ref, ref, sem).wait()

    pending = []

    class Send:
        def __init__(self, src, dst, send, recv, device, local=None, only=None):
            self.ends = (src, dst, recv)
            self.copy = remote(src, dst, send, recv, device)
            self.local, self.only = local, only

        def start(self):
            if self.only is not None:
                pl.when(self.only)(self.copy.start)
            elif self.local is None:
                self.copy.start()
            else:
                pl.when(self.local)(lambda: pltpu.make_async_copy(*self.ends).start())
                pl.when(jnp.logical_not(self.local))(self.copy.start)

        def wait(self):
            if self.only is not None:
                pl.when(self.only)(self.copy.wait_send)
            elif self.local is None:
                self.copy.wait_send()
            else:
                pl.when(jnp.logical_not(self.local))(self.copy.wait_send)

    def spread(src_of, dst, recv, kind):
        sends = []
        for step in range(heads):
            which = lax.rem(head + step, heads)
            sends.append(Send(
                src_of(which), dst, s_in.at[kind, step], recv, place(home_block, which),
                stays if step == 0 else None,
            ))
        return sends

    def feed(after, sends):
        sends = list(sends)
        for done in after:
            done.wait()
            if sends:
                sends.pop(0).start()
        for send in sends:
            send.start()

    stride = heads // groups
    shift = lax.rem(part + 2 * groups * heads - home_slot - head, groups)
    w_sends = []
    for step in range(stride):
        offset = shift + groups * step
        which = lax.rem(head + offset, heads)
        w_sends.append(Send(
            w_in.at[which], wb.at[me], s_in.at[4, step], r_w.at[me], place(home_block, which),
            (offset == 0) & stays if step == 0 else None,
        ))
    feed([], w_sends)
    k_sends = spread(lambda w: kvq_in.at[w, 0], kv.at[home_slot, 0], r_k.at[home_slot], 0)
    feed([], k_sends)
    if CROSS:
        loads[3].wait()
        flip(2, q_in)
    x_sends = []
    for step in range(CROSS):
        which = lax.rem(head + step, CROSS)
        x_sends.append(Send(
            kvq_in.at[which, 2], qx.at[home_slot], s_x.at[step], r_x.at[home_slot],
            place(jnp.maximum(home_block - 1, 0), which), only=home_block > 0,
        ))
    feed([], x_sends)
    first = lax.rem(part + groups * heads - head, groups)

    def share_weights(slot, t, k, to_part, to_member):
        copy = remote(wb.at[slot], wb.at[slot], s_wf.at[t, k], r_w.at[slot], place(to_member, head), to_part)
        copy.start()
        pending.append(copy)

    for t in range(stride):
        slot = base + first + groups * t
        landed(wb.at[slot], r_w.at[slot])
        for d in range(1, group):
            share_weights(slot, t, d, part, lax.rem(member + d, group))
        for other in range(1, groups):
            share_weights(slot, t, other * group, lax.rem(part + other, groups), member)

    loads[2].wait()
    flip(1, v_in)
    v_sends = spread(lambda w: kvq_in.at[w, 1], kv.at[home_slot, 1], r_v.at[home_slot], 1)
    st_sends = spread(lambda w: step_in, stb.at[home_slot], r_st.at[home_slot], 2)
    feed(k_sends if GATE == 0 else [], v_sends)
    feed([], st_sends)
    if not CROSS:
        loads[3].wait()
        flip(2, q_in)
    q_sends = spread(lambda w: kvq_in.at[w, 2], qb.at[home_slot], r_q.at[home_slot], 3)
    for h in range(heads):
        @pl.when(head == h)
        def _():
            at = slice(h * width, (h + 1) * width)
            for m, gain in enumerate((fast_gain, window_gain)):
                gain_cols[m] = jnp.broadcast_to(gain[at].reshape(1, width), (LANES, width)).T

    for i in range(heads):
        landed(kv.at[i, 0], r_k.at[i])
        kn[i * LANES : (i + 1) * LANES, :] = kv[i, 0].T
    for d in range(1, group):
        for t in range(stride):
            slot = lax.rem(member + d, group) * heads + first + groups * t
            landed(wb.at[slot], r_w.at[slot])
            for other in range(1, groups):
                share_weights(slot, t, other * group + d, lax.rem(part + other, groups), member)
    feed(v_sends if GATE == 0 else k_sends if GATE == 1 else [], q_sends)
    key_at = lax.broadcasted_iota(jnp.int32, (span, chunk), 0)
    lane_at = lax.broadcasted_iota(jnp.int32, (1, chunk), 1)

    def soften(scores, values):
        top = jnp.max(scores, axis=0, keepdims=True)
        powers = jnp.exp(scores - top)
        total = jnp.sum(powers, axis=0, keepdims=True)
        probs = (powers * (1.0 / total)).astype(BF16)
        return dot(values, probs), jnp.broadcast_to(top + jnp.log(total), (8, chunk))

    def normalize(field, gain):
        mean_sq = jnp.mean(field * field, axis=0, keepdims=True)
        return field * lax.rsqrt(mean_sq + 1e-05) * gain

    up_there = place(jnp.minimum(member + 1, group - 1), head)
    down_there = place(jnp.maximum(member - 1, 0), head)

    def passed(slot):
        return Send(
            qb.at[slot], qx.at[slot], s_xf.at[slot], r_x.at[slot], down_there,
            only=above if paired is None else paired & above,
        )

    def raised(slot):
        return (
            remote(xo_stage.at[slot], xo.at[slot], s_xo.at[slot], r_xo.at[slot], up_there),
            remote(xl_stage.at[slot], xl.at[slot], s_xl.at[slot], r_xl.at[slot], up_there),
        )

    def cross(c):
        start = c * chunk
        for slot in (2 * c, 2 * c + 1):
            landed(qx.at[slot], r_x.at[slot])
        query = jnp.concatenate([qx[2 * c], qx[2 * c + 1]], axis=1)
        scores = dot(kn[start:, :], query) * scale
        scores = jnp.where(key_at[start:] > lane_at + start, scores, -1e30)
        field, level = soften(scores, vt[:, start:])
        for half in range(2):
            slot = 2 * c + half
            there = slice(half * LANES, (half + 1) * LANES)
            xo_stage[slot] = field[:, there].astype(BF16)
            xl_stage[slot] = level[:, there]
            for copy in raised(slot):
                copy.start()

    def values_land():
        for i in range(heads):
            landed(kv.at[i, 1], r_v.at[i])
            there = slice(i * LANES, (i + 1) * LANES)
            vt[:, there] = kv[i, 1]

    if CROSS:
        values_land()

        @pl.when(below if paired is None else below & jnp.logical_not(paired))
        def _():
            for c in range(chunks):
                cross(c)

    for d in range(group):
        for e in range(1, groups):
            for t in range(stride):
                slot = lax.rem(member + d, group) * heads + lax.rem(first + e, groups) + groups * t
                landed(wb.at[slot], r_w.at[slot])
    for s in range(n):
        piece = wb[s].astype(F32)
        for m in range(3):
            wfull[m, s * rows : (s + 1) * rows, :] = piece[m * rows : (m + 1) * rows, :]
    for m in range(3):
        wbf[m] = wfull[m].astype(BF16)

    def gate_chunk(c, carry):
        there = pl.ds(pl.multiple_of(c * chunk, chunk), chunk)
        keys = jnp.concatenate([kv[2 * c, 0], kv[2 * c + 1, 0]], axis=1)
        gates[:, there] = dot_tn(wbf[0], keys) * scale
        ups[:, there] = dot_tn(wbf[1], keys) * scale
        return carry

    lax.fori_loop(0, chunks, gate_chunk, 0)

    if not CROSS:
        values_land()
    for i in range(heads):
        landed(stb.at[i], r_st.at[i])
        there = slice(i * LANES, (i + 1) * LANES)
        tgt[:, there] = (-stb[i, pl.ds(head, 1), :] * kv[i, 1].astype(F32)).astype(BF16)


    def grad_chunk(c, carry):
        there = pl.ds(pl.multiple_of(c * chunk, chunk), chunk)
        gate = gates[:, there]
        up = ups[:, there]
        back = dot(wbf[2], tgt[:, there]) * scale
        sigma = jax.nn.sigmoid(gate)
        silu = gate * sigma
        hid[:, there] = (silu * up).astype(BF16)
        gg[:, there] = (back * up * (sigma * (1.0 + gate * (1.0 - sigma)))).astype(BF16)
        gu[:, there] = (back * silu).astype(BF16)
        return carry

    lax.fori_loop(0, chunks, grad_chunk, 0)
    own_keys = jnp.concatenate([kv[i, 0] for i in range(heads)], axis=1)
    for m, (left, right) in enumerate(((own_keys, gg), (own_keys, gu), (hid[...], tgt))):
        grad = dot_nt(left, right[...]) * scale
        for s in range(n):
            gstage[s // heads, s % heads, m * rows : (m + 1) * rows, :] = grad[s * rows : (s + 1) * rows, :]

    for d in range(1, group):
        other = lax.rem(member + d, group)
        for i in range(heads):
            gother[d - 1, i] = gstage[other, i].astype(BF16)
        copy = remote(gother.at[d - 1], ginc.at[d - 1], s_gp.at[d - 1], r_gp.at[d - 1], place(other, head))
        copy.start()
        pending.append(copy)

    def attend(c):
        reach = (c + 1) * chunk
        query = jnp.concatenate([qb[2 * c], qb[2 * c + 1]], axis=1)
        scores = dot(kn[:reach, :], query) * scale
        scores = jnp.where(key_at[:reach] <= lane_at + c * chunk, scores, -1e30)
        attended, level = soften(scores, vt[:, :reach])
        gate = dot_tn(wbf[0], query) * scale
        up = dot_tn(wbf[1], query) * scale
        hidden = (gate * jax.nn.sigmoid(gate) * up).astype(BF16)
        fast = dot_tn(wbf[2], hidden) * scale
        for half in range(2):
            there = slice(half * LANES, (half + 1) * LANES)
            own_o[2 * c + half] = attended[:, there]
            own_l[2 * c + half] = level[:, there]
            fast_o[2 * c + half] = normalize(fast[:, there], gain_cols[0])

    def result_of(slot):
        dst = out.at[pl.ds(pl.multiple_of(head * width, 64), width), :]
        return Send(ostage.at[slot], dst, s_o.at[slot], r_o.at[head], base + slot, base + slot == me)

    def finalize(slot):
        @pl.when(above)
        def _():
            landed(xo.at[slot], r_xo.at[slot])
            landed(xl.at[slot], r_xl.at[slot])
            here = own_l[slot, 0:1, :]
            there = xl[slot, 0:1, :]
            share = 1.0 / (1.0 + jnp.exp(there - here))
            rest = 1.0 / (1.0 + jnp.exp(here - there))
            own_o[slot] = own_o[slot] * share + xo[slot].astype(F32) * rest

        ostage[slot] = (fast_o[slot] + normalize(own_o[slot], gain_cols[1])).astype(BF16)
        result_of(slot).start()

    def g_sends(src_of, dst, send, recv):
        sends = []
        for step in range(heads):
            i = lax.rem(home_slot + step, heads)
            sends.append(Send(src_of(i), dst.at[head], send.at[step], recv.at[head], base + i, stays if step == 0 else None))
        return sends

    def partner_sums():
        return [
            remote(sums, sinc.at[d - 1], s_sp.at[d - 1], r_sp.at[d - 1], place(lax.rem(member + d, group), head))
            for d in range(1, group)
        ]

    def gather_gradient():
        for d in range(1, group):
            landed(ginc.at[d - 1], r_gp.at[d - 1])
        sums[...] = jnp.zeros_like(sums)

        def add_up(i, carry):
            total = gstage[member, i]
            for d in range(1, group):
                total = total + ginc[d - 1, i].astype(F32)
            gsend[i] = total.astype(BF16)
            weight = wb[base + i].astype(F32)
            moved = weight - total
            for m in range(3):
                piece = slice(m * rows, (m + 1) * rows)
                old = weight[piece, :]
                new = moved[piece, :]
                sums[m : m + 1, :] += jnp.sum(old * old, axis=0, keepdims=True)
                sums[4 + m : 5 + m, :] += jnp.sum(new * new, axis=0, keepdims=True)
            return carry

        lax.fori_loop(0, heads, add_up, 0)
        for copy in partner_sums():
            copy.start()
        if not G_LATE:
            send_gradient()

    def send_gradient():
        for send in g_sends(lambda i: gsend.at[i], g_out, s_g, r_g):
            send.start()

    def send_scales():
        for d in range(1, group):
            landed(sinc.at[d - 1], r_sp.at[d - 1])
        total = sums[...]
        for d in range(1, group):
            total = total + sinc[d - 1]
        scale_send[0:4, :] = jnp.sqrt((total[0:4] + 1e-06) / (total[4:8] + 1e-06))
        scale_send[4:8, :] = total[4:8]
        for send in g_sends(lambda i: scale_send, scale_out, s_sc, r_sc):
            send.start()

    late = member >= 0
    if near:
        if CROSS:
            late = jnp.logical_not(paired)
            early = paired
        else:
            early = member >= 0
            late = member < 0

        @pl.when(early)
        def _():
            gather_gradient()
            send_scales()

    turn = head % chunks
    if near:
        for t in range(heads):
            slot = lax.rem(2 * turn + t, heads)
            landed(qb.at[slot], r_q.at[slot])
            passed(slot).start()
        if G_LATE:
            send_gradient()
    else:
        for slot in range(heads):
            landed(qb.at[slot], r_q.at[slot])

    def work(t, carry):
        now = lax.rem(turn + t, chunks)
        for c in range(chunks):
            @pl.when(now == c)
            def _():
                if near:
                    pl.when(below if paired is None else below & paired)(lambda: cross(c))
                attend(c)

        if GATHER_AT < chunks:
            pl.when(late & (t == GATHER_AT))(gather_gradient)
        if GATHER_AT + 1 < chunks:
            pl.when(late & (t == GATHER_AT + 1))(send_scales)
        if LAG:
            @pl.when(t > 0)
            def _():
                before = lax.rem(turn + t + chunks - 1, chunks)
                finalize(2 * before)
                finalize(2 * before + 1)
        else:
            finalize(2 * now)
            finalize(2 * now + 1)
        return carry

    lax.fori_loop(0, chunks, work, 0)
    if GATHER_AT + 1 >= chunks:
        @pl.when(late)
        def _():
            if GATHER_AT >= chunks:
                gather_gradient()
            send_scales()
    if LAG:
        last = lax.rem(turn + chunks - 1, chunks)
        finalize(2 * last)
        finalize(2 * last + 1)

    for copy in pending:
        copy.wait_send()
    for send in w_sends + st_sends + x_sends + q_sends + (v_sends if GATE else []) + (k_sends if GATE == 2 else []):
        send.wait()
    for send in g_sends(lambda i: gsend.at[i], g_out, s_g, r_g) + g_sends(lambda i: scale_send, scale_out, s_sc, r_sc):
        send.wait()
    for copy in partner_sums():
        copy.wait_send()
    if near:
        for slot in range(heads):
            passed(slot).wait()

    @pl.when(below)
    def _():
        for slot in range(heads):
            for copy in raised(slot):
                copy.wait_send()

    for h in range(heads):
        landed(g_out.at[h], r_g.at[h])
        landed(scale_out.at[h], r_sc.at[h])
        landed(out.at[pl.ds(h * width, width), :], r_o.at[h])
    for slot in range(heads):
        result_of(slot).wait()


def finish(heads, width, rows, out_t, grads, scales, weights, layer_out, new_weights, momentum):
    layer_out[...] = out_t[...].T
    for h in range(heads):
        grad = grads[h].astype(F32)
        for m in range(3):
            at = (m * heads + h) * width
            part = grad[m * rows : (m + 1) * rows, :]
            momentum[:, at : at + width] = part
            new_weights[:, at : at + width] = (weights[:, at : at + width] - part) * scales[h, m : m + 1, :]


def shards(queries, key_vectors, value_vectors, step_sizes, fast_weights, fast_gain, window_gain):
    tokens = queries.shape[0]
    heads = step_sizes.shape[1]
    width = queries.shape[1] // heads
    n = lax.axis_size("seq")
    groups = lax.axis_size("groups")
    group = n // heads
    rows = width // n
    assert tokens == LANES and heads * tokens == WINDOW and group % 2 == 0
    span = heads * LANES
    vmem = pl.BlockSpec(memory_space=pltpu.VMEM)
    hbm = pl.BlockSpec(memory_space=pl.ANY)
    dma = pltpu.SemaphoreType.DMA
    more = max(group - 1, 1)
    token_piece = pltpu.VMEM((heads, width, LANES), BF16)
    level_piece = pltpu.VMEM((heads, 8, LANES), F32)
    weight_piece = pltpu.VMEM((heads, 3 * rows, width), BF16)
    across = pltpu.VMEM((width, span), BF16)
    across_wide = pltpu.VMEM((width, span), F32)
    out_t, grads, scales = pl.pallas_call(
        functools.partial(kernel, n, groups, heads, width),
        out_shape=(
            jax.ShapeDtypeStruct((heads * width, LANES), BF16),
            jax.ShapeDtypeStruct((heads, 3 * rows, width), BF16),
            jax.ShapeDtypeStruct((heads, 8, width), F32),
        ),
        in_specs=[hbm, hbm, hbm, vmem, hbm, vmem, vmem],
        out_specs=(vmem, vmem, vmem),
        scratch_shapes=[
            pltpu.VMEM(queries.shape, BF16),
            pltpu.VMEM(queries.shape, BF16),
            pltpu.VMEM(queries.shape, BF16),
            pltpu.VMEM(fast_weights.shape, F32),
            dma((4,)),
            pltpu.VMEM((heads, 3, width, LANES), BF16),
            weight_piece,
            pltpu.VMEM((heads, 3 * rows, width), F32),
            pltpu.VMEM((heads, 2, width, LANES), BF16),
            token_piece,
            token_piece,
            pltpu.VMEM((heads, heads, LANES), F32),
            pltpu.VMEM((n, 3 * rows, width), BF16),
            pltpu.VMEM((3, width, width), F32),
            pltpu.VMEM((3, width, width), BF16),
            pltpu.VMEM((span, width), BF16),
            across,
            across_wide, across_wide, across, across, across, across,
            pltpu.VMEM((group, heads, 3 * rows, width), F32),
            pltpu.VMEM((more, heads, 3 * rows, width), BF16),
            pltpu.VMEM((more, heads, 3 * rows, width), BF16),
            weight_piece,
            pltpu.VMEM((8, width), F32),
            pltpu.VMEM((more, 8, width), F32),
            pltpu.VMEM((8, width), F32),
            token_piece,
            pltpu.VMEM((2, width, LANES), F32),
            pltpu.VMEM((heads, width, LANES), F32),
            level_piece,
            pltpu.VMEM((heads, width, LANES), F32),
            token_piece,
            level_piece,
            token_piece,
            level_piece,
            dma((5, heads)), dma((heads,)), dma((heads,)), dma((heads,)), dma((heads,)), dma((heads,)), dma((n,)),
            dma((heads // groups, groups * group)), dma((heads,)), dma((heads,)),
            dma((heads,)), dma((heads,)), dma((heads,)), dma((heads,)),
            dma((more,)), dma((more,)), dma((more,)), dma((more,)),
            dma((heads,)), dma((heads,)), dma((heads,)), dma((heads,)), dma((heads,)), dma((heads,)),
        ],
        compiler_params=pltpu.CompilerParams(
            collective_id=0, has_side_effects=True, vmem_limit_bytes=60 << 20
        ),
        name="ttt",
    )(key_vectors, value_vectors, queries, step_sizes.T, fast_weights, fast_gain, window_gain)
    return pl.pallas_call(
        functools.partial(finish, heads, width, rows),
        out_shape=(
            jax.ShapeDtypeStruct(queries.shape, BF16),
            jax.ShapeDtypeStruct(fast_weights.shape, F32),
            jax.ShapeDtypeStruct(fast_weights.shape, F32),
        ),
        in_specs=[vmem] * 4,
        out_specs=(vmem, vmem, vmem),
        name="finish",
    )(out_t, grads, scales, fast_weights)


def solution(mesh):
    in_specs = (
        P(("groups", "seq"), None),
        P(("groups", "seq"), None),
        P(("groups", "seq"), None),
        P(("groups", "seq"), None),
        P("seq", None),
        P(),
        P(),
    )
    out_specs = (P(("groups", "seq"), None), P(("groups", "seq"), None), P(("groups", "seq"), None))
    return jax.shard_map(shards, mesh=mesh, in_specs=in_specs, out_specs=out_specs, check_vma=False)
```

```python
import functools
import math

import jax
import jax.numpy as jnp
from jax import lax
from jax.experimental import pallas as pl
from jax.experimental.pallas import tpu as pltpu
from jax.sharding import PartitionSpec as P

WINDOW = 1024
LANES = 128
F32 = jnp.float32
BF16 = jnp.bfloat16


def dot(a, b):
    return jnp.dot(a, b, preferred_element_type=F32)


def dot_nt(a, b):
    return lax.dot_general(a, b, (((1,), (1,)), ((), ())), preferred_element_type=F32)


def dot_tn(a, b):
    return lax.dot_general(a, b, (((0,), (0,)), ((), ())), preferred_element_type=F32)


def packing(rows):
    tall = -(-3 * rows // 16) * 16
    rest = -(-3 * rows // 32) * 16
    return tall, rest


def pack(dst, src, rows):
    tall, rest = packing(rows)
    dst[:tall, :] = src[:tall, :LANES].astype(BF16)
    dst[tall : 2 * tall, :] = src[:tall, LANES : 2 * LANES].astype(BF16)
    sides = [src[:rest, 2 * LANES :], src[rest : 2 * rest, 2 * LANES :]]
    dst[2 * tall :, :] = jnp.concatenate(sides, axis=1).astype(BF16)


def unpack(packed, rows):
    tall, rest = packing(rows)
    packed = packed.astype(F32)
    last = packed[2 * tall :]
    last = jnp.concatenate([last[:, : LANES // 2], last[:, LANES // 2 :]], axis=0)
    return jnp.concatenate([packed[:tall], packed[tall : 2 * tall], last[:tall]], axis=1)


def kernel(
    n, groups, heads, width,
    k_hbm, v_hbm, q_hbm, step_in, w_hbm, fast_gain, window_gain,
    out, g_out, scale_out,
    k_in, v_in, q_in, weights, s_load,
    kvq_in, w_in, wide,
    kv, qb, qx, stb, wb, wfull, wbf, kn, vt, gates, ups, hid, tgt, gg, gu,
    gstage, gother, ginc, gsend, sums, sinc, scale_send, ostage, gain_cols,
    own_o, own_l, fast_o, xo_stage, xl_stage, xo, xl,
    s_in, r_k, r_v, r_q, r_x, r_st, r_w,
    s_wf, s_xf, s_xo, s_xl, r_xo, r_xl,
    s_gp, r_gp, s_sp, r_sp, s_g, r_g, s_sc, r_sc, s_o, r_o,
):
    group = n // heads
    rows = width // n
    span = heads * LANES
    chunk = 2 * LANES
    chunks = span // chunk
    scale = 1.0 / math.sqrt(width)
    me = lax.axis_index("seq")
    part = lax.axis_index("groups")
    home_block = me // heads
    home_slot = me % heads
    quarter = heads // 2
    spot = me % (2 * heads)
    pair = me // (2 * heads)
    head = spot // 2
    member = 2 * pair + spot % 2
    half = home_block % 2
    local = head // quarter == member % 2

    def place(block, which):
        odd = block % 2
        return (block - odd) * heads + 2 * which + odd

    base = member * heads
    below = member < group - 1
    above = member > 0
    stays = member == home_block

    def remote(src, dst, send, recv, device, to_part=None):
        return pltpu.make_async_remote_copy(
            src_ref=src, dst_ref=dst, send_sem=send, recv_sem=recv,
            device_id={"groups": part if to_part is None else to_part, "seq": device},
            device_id_type=pl.DeviceIdType.MESH,
        )

    loads = [
        pltpu.make_async_copy(src, dst, s_load.at[i])
        for i, (src, dst) in enumerate(((w_hbm, weights), (k_hbm, k_in), (v_hbm, v_in), (q_hbm, q_in)))
    ]
    for load in loads:
        load.start()
    barrier = pltpu.get_barrier_semaphore()
    for step in range(1, n):
        pl.semaphore_signal(
            barrier, inc=1, device_id={"seq": lax.rem(me + step, n)},
            device_id_type=pl.DeviceIdType.MESH,
        )
    for other in range(1, groups):
        for d in range(group):
            pl.semaphore_signal(
                barrier, inc=1,
                device_id={"groups": lax.rem(part + other, groups), "seq": place(d, head)},
                device_id_type=pl.DeviceIdType.MESH,
            )

    def flip(m, ref):
        for h in range(0, heads, 2):
            both = ref[:, h * width : (h + 2) * width].T
            kvq_in[h, m] = both[:width]
            kvq_in[h + 1, m] = both[width:]

    loads[0].wait()
    for h in range(heads):
        for m in range(3):
            at = (m * heads + h) * width
            wide[h, m * rows : (m + 1) * rows, :] = weights[:, at : at + width]
        pack(w_in.at[h], wide.at[h], rows)
    loads[1].wait()
    flip(0, k_in)
    pl.semaphore_wait(barrier, n - 1 + (groups - 1) * group)

    def landed(ref, sem):
        pltpu.make_async_copy(ref, ref, sem).wait()

    pending = []

    class Send:
        def __init__(self, src, dst, send, recv, device, local=None, only=None):
            self.ends = (src, dst, recv)
            self.copy = remote(src, dst, send, recv, device)
            self.local, self.only = local, only

        def start(self):
            if self.only is not None:
                pl.when(self.only)(self.copy.start)
            elif self.local is None:
                self.copy.start()
            else:
                pl.when(self.local)(lambda: pltpu.make_async_copy(*self.ends).start())
                pl.when(jnp.logical_not(self.local))(self.copy.start)

        def wait(self):
            if self.only is not None:
                pl.when(self.only)(self.copy.wait_send)
            elif self.local is None:
                self.copy.wait_send()
            else:
                pl.when(jnp.logical_not(self.local))(self.copy.wait_send)

    def spread(src_of, dst, recv, kind):
        sends = []
        for step in range(heads):
            which = lax.rem(head + step, heads)
            sends.append(Send(
                src_of(which), dst, s_in.at[kind, step], recv, place(home_block, which),
                stays if step == 0 else None,
            ))
        return sends

    def feed(after, sends):
        sends = list(sends)
        for done in after:
            done.wait()
            if sends:
                sends.pop(0).start()
        for send in sends:
            send.start()

    stride = heads // groups
    shift = lax.rem(part + 2 * groups * heads - home_slot - head, groups)
    w_sends = []
    for step in range(stride):
        offset = shift + groups * step
        which = lax.rem(head + offset, heads)
        w_sends.append(Send(
            w_in.at[which], wb.at[me], s_in.at[4, step], r_w.at[me], place(home_block, which),
            (offset == 0) & stays if step == 0 else None,
        ))
    feed([], w_sends)
    k_sends = spread(lambda w: kvq_in.at[w, 0], kv.at[home_slot, 0], r_k.at[home_slot], 0)
    feed([], k_sends)
    loads[2].wait()
    flip(1, v_in)
    v_sends = spread(lambda w: kvq_in.at[w, 1], kv.at[home_slot, 1], r_v.at[home_slot], 1)
    st_sends = spread(lambda w: step_in, stb.at[home_slot], r_st.at[home_slot], 2)
    feed([], v_sends + st_sends)
    loads[3].wait()
    flip(2, q_in)
    q_sends = spread(lambda w: kvq_in.at[w, 2], qb.at[home_slot], r_q.at[home_slot], 3)
    feed([], q_sends)
    first = lax.rem(part + groups * heads - head, groups)

    def share_weights(slot, t, k, to_part, to_member):
        copy = remote(wb.at[slot], wb.at[slot], s_wf.at[t, k], r_w.at[slot], place(to_member, head), to_part)
        copy.start()
        pending.append(copy)

    for t in range(stride):
        slot = base + first + groups * t
        landed(wb.at[slot], r_w.at[slot])
        for d in range(1, group):
            share_weights(slot, t, d, part, lax.rem(member + d, group))
        for other in range(1, groups):
            share_weights(slot, t, other * group, lax.rem(part + other, groups), member)

    for h in range(heads):
        @pl.when(head == h)
        def _():
            at = slice(h * width, (h + 1) * width)
            for m, gain in enumerate((fast_gain, window_gain)):
                gain_cols[m] = jnp.broadcast_to(gain[at].reshape(1, width), (LANES, width)).T

    for d in range(1, group):
        for t in range(stride):
            slot = lax.rem(member + d, group) * heads + first + groups * t
            landed(wb.at[slot], r_w.at[slot])
            for other in range(1, groups):
                share_weights(slot, t, other * group + d, lax.rem(part + other, groups), member)
    key_at = lax.broadcasted_iota(jnp.int32, (span, chunk), 0)
    lane_at = lax.broadcasted_iota(jnp.int32, (1, chunk), 1)

    def soften(scores, values):
        top = jnp.max(scores, axis=0, keepdims=True)
        powers = jnp.exp(scores - top)
        total = jnp.sum(powers, axis=0, keepdims=True)
        probs = (powers * (1.0 / total)).astype(BF16)
        return dot(values, probs), jnp.broadcast_to(top + jnp.log(total), (8, chunk))

    def normalize(field, gain):
        mean_sq = jnp.mean(field * field, axis=0, keepdims=True)
        return field * lax.rsqrt(mean_sq + 1e-05) * gain

    up_there = place(jnp.minimum(member + 1, group - 1), head)
    down_there = place(jnp.maximum(member - 1, 0), head)

    def passed(slot):
        return Send(qb.at[slot], qx.at[slot], s_xf.at[slot], r_x.at[slot], down_there, only=above)

    def raised(slot):
        return (
            remote(xo_stage.at[slot], xo.at[slot], s_xo.at[slot], r_xo.at[slot], up_there),
            remote(xl_stage.at[slot], xl.at[slot], s_xl.at[slot], r_xl.at[slot], up_there),
        )

    def cross(c):
        start = c * chunk
        for slot in (2 * c, 2 * c + 1):
            landed(qx.at[slot], r_x.at[slot])
        query = jnp.concatenate([qx[2 * c], qx[2 * c + 1]], axis=1)
        scores = dot(kn[start:, :], query) * scale
        scores = jnp.where(key_at[start:] > lane_at + start, scores, -1e30)
        field, level = soften(scores, vt[:, start:])
        for half in range(2):
            slot = 2 * c + half
            there = slice(half * LANES, (half + 1) * LANES)
            xo_stage[slot] = field[:, there].astype(BF16)
            xl_stage[slot] = level[:, there]
            for copy in raised(slot):
                copy.start()

    def gate_chunk(c, carry):
        there = pl.ds(pl.multiple_of(c * chunk, chunk), chunk)
        keys = jnp.concatenate([kv[2 * c, 0], kv[2 * c + 1, 0]], axis=1)
        gates[:, there] = dot_tn(wbf[0], keys) * scale
        ups[:, there] = dot_tn(wbf[1], keys) * scale
        return carry

    def grad_chunk(c, carry):
        there = pl.ds(pl.multiple_of(c * chunk, chunk), chunk)
        gate = gates[:, there]
        up = ups[:, there]
        back = dot(wbf[2], tgt[:, there]) * scale
        sigma = jax.nn.sigmoid(gate)
        silu = gate * sigma
        hid[:, there] = (silu * up).astype(BF16)
        gg[:, there] = (back * up * (sigma * (1.0 + gate * (1.0 - sigma)))).astype(BF16)
        gu[:, there] = (back * silu).astype(BF16)
        return carry

    def gother_sends():
        return [
            remote(
                gother.at[d - 1], ginc.at[d - 1], s_gp.at[d - 1], r_gp.at[d - 1],
                place(lax.rem(member + d, group), head),
            )
            for d in range(1, group)
        ]

    def learn():
        for i in range(heads):
            landed(kv.at[i, 0], r_k.at[i])
            kn[i * LANES : (i + 1) * LANES, :] = kv[i, 0].T
        for d in range(group):
            for e in range(1, groups):
                for t in range(stride):
                    slot = lax.rem(member + d, group) * heads + lax.rem(first + e, groups) + groups * t
                    landed(wb.at[slot], r_w.at[slot])
        for s in range(n):
            piece = unpack(wb[s], rows)
            for m in range(3):
                wfull[m, s * rows : (s + 1) * rows, :] = piece[m * rows : (m + 1) * rows, :]
        for m in range(3):
            wbf[m] = wfull[m].astype(BF16)
        lax.fori_loop(0, chunks, gate_chunk, 0)
        for i in range(heads):
            landed(kv.at[i, 1], r_v.at[i])
            landed(stb.at[i], r_st.at[i])
            there = slice(i * LANES, (i + 1) * LANES)
            vt[:, there] = kv[i, 1]
            tgt[:, there] = (-stb[i, pl.ds(head, 1), :] * kv[i, 1].astype(F32)).astype(BF16)
        lax.fori_loop(0, chunks, grad_chunk, 0)
        own_keys = jnp.concatenate([kv[i, 0] for i in range(heads)], axis=1)
        for m, (left, right) in enumerate(((own_keys, gg), (own_keys, gu), (hid[...], tgt))):
            grad = dot_nt(left, right[...]) * scale
            for s in range(n):
                gstage[s // heads, s % heads, m * rows : (m + 1) * rows, :] = grad[s * rows : (s + 1) * rows, :]
        for d in range(1, group):
            other = lax.rem(member + d, group)
            for i in range(heads):
                gother[d - 1, i] = gstage[other, i, : 3 * rows, :].astype(BF16)
        for copy in gother_sends():
            copy.start()

    def attend(c):
        reach = (c + 1) * chunk
        query = jnp.concatenate([qb[2 * c], qb[2 * c + 1]], axis=1)
        scores = dot(kn[:reach, :], query) * scale
        scores = jnp.where(key_at[:reach] <= lane_at + c * chunk, scores, -1e30)
        attended, level = soften(scores, vt[:, :reach])
        gate = dot_tn(wbf[0], query) * scale
        up = dot_tn(wbf[1], query) * scale
        hidden = (gate * jax.nn.sigmoid(gate) * up).astype(BF16)
        fast = dot_tn(wbf[2], hidden) * scale
        for half in range(2):
            there = slice(half * LANES, (half + 1) * LANES)
            own_o[2 * c + half] = attended[:, there]
            own_l[2 * c + half] = level[:, there]
            fast_o[2 * c + half] = normalize(fast[:, there], gain_cols[0])

    def result_of(slot):
        dst = out.at[pl.ds(pl.multiple_of(head * width, 64), width), :]
        return Send(ostage.at[slot], dst, s_o.at[slot], r_o.at[head], base + slot, base + slot == me)

    def finalize(slot):
        @pl.when(above)
        def _():
            landed(xo.at[slot], r_xo.at[slot])
            landed(xl.at[slot], r_xl.at[slot])
            here = own_l[slot, 0:1, :]
            there = xl[slot, 0:1, :]
            share = 1.0 / (1.0 + jnp.exp(there - here))
            rest = 1.0 / (1.0 + jnp.exp(here - there))
            own_o[slot] = own_o[slot] * share + xo[slot].astype(F32) * rest

        ostage[slot] = (fast_o[slot] + normalize(own_o[slot], gain_cols[1])).astype(BF16)
        result_of(slot).start()

    def g_sends(src_of, dst, send, recv):
        sends = []
        for step in range(heads):
            i = lax.rem(home_slot + step, heads)
            sends.append(Send(src_of(i), dst.at[head], send.at[step], recv.at[head], base + i, stays if step == 0 else None))
        return sends

    def partner_sums():
        return [
            remote(sums, sinc.at[d - 1], s_sp.at[d - 1], r_sp.at[d - 1], place(lax.rem(member + d, group), head))
            for d in range(1, group)
        ]

    def gather_gradient():
        for d in range(1, group):
            landed(ginc.at[d - 1], r_gp.at[d - 1])
        sums[...] = jnp.zeros_like(sums)

        def add_up(i, carry):
            total = gstage[member, i, : 3 * rows, :]
            for d in range(1, group):
                total = total + ginc[d - 1, i].astype(F32)
            gstage[member, i, : 3 * rows, :] = total
            pack(gsend.at[i], gstage.at[member, i], rows)
            weight = unpack(wb[base + i], rows)[: 3 * rows]
            moved = weight - total
            for m in range(3):
                piece = slice(m * rows, (m + 1) * rows)
                old = weight[piece, :]
                new = moved[piece, :]
                sums[m : m + 1, :] += jnp.sum(old * old, axis=0, keepdims=True)
                sums[4 + m : 5 + m, :] += jnp.sum(new * new, axis=0, keepdims=True)
            return carry

        lax.fori_loop(0, heads, add_up, 0)
        for copy in partner_sums():
            copy.start()
        for send in g_sends(lambda i: gsend.at[i], g_out, s_g, r_g):
            send.start()

    def send_scales():
        for d in range(1, group):
            landed(sinc.at[d - 1], r_sp.at[d - 1])
        total = sums[...]
        for d in range(1, group):
            total = total + sinc[d - 1]
        ratio = jnp.sqrt((total[0:4] + 1e-06) / (total[4:8] + 1e-06))
        for m in range(3):
            scale_send[2 * m : 2 * m + 1, :] = ratio[m : m + 1, :LANES]
            scale_send[2 * m + 1 : 2 * m + 2, :] = ratio[m : m + 1, LANES : 2 * LANES]
        scale_send[6:7, :] = jnp.concatenate([ratio[0:1, 2 * LANES :], ratio[1:2, 2 * LANES :]], axis=1)
        scale_send[7:8, :] = jnp.concatenate([ratio[2:3, 2 * LANES :], ratio[2:3, 2 * LANES :]], axis=1)
        for send in g_sends(lambda i: scale_send, scale_out, s_sc, r_sc):
            send.start()

    turn = head % chunks

    def each_chunk(act):
        def body(t, carry):
            act(lax.rem(turn + t, chunks))
            return carry

        lax.fori_loop(0, chunks, body, 0)

    def choose(act, now):
        for c in range(chunks):
            pl.when(now == c)(functools.partial(act, c))

    def finish_chunk(now):
        finalize(2 * now)
        finalize(2 * now + 1)

    def attend_chunk(now):
        choose(attend, now)
        pl.when(jnp.logical_not(local & above))(lambda: finish_chunk(now))

    def attend_all():
        for t in range(heads):
            slot = lax.rem(2 * turn + t, heads)
            landed(qb.at[slot], r_q.at[slot])
            passed(slot).start()
        each_chunk(attend_chunk)

    def cross_all():
        each_chunk(lambda now: choose(cross, now))

    learn()
    gather_gradient()
    send_scales()
    pl.when(below & jnp.logical_not(local))(cross_all)
    attend_all()
    pl.when(below & local)(cross_all)

    @pl.when(local & above)
    def _():
        each_chunk(finish_chunk)

    for copy in pending:
        copy.wait_send()
    for send in w_sends + st_sends + k_sends + v_sends + q_sends:
        send.wait()
    for send in g_sends(lambda i: gsend.at[i], g_out, s_g, r_g) + g_sends(lambda i: scale_send, scale_out, s_sc, r_sc):
        send.wait()
    for copy in partner_sums() + gother_sends():
        copy.wait_send()
    for slot in range(heads):
        passed(slot).wait()

    @pl.when(below)
    def _():
        for slot in range(heads):
            for copy in raised(slot):
                copy.wait_send()

    for h in range(heads):
        landed(g_out.at[h], r_g.at[h])
        landed(scale_out.at[h], r_sc.at[h])
        landed(out.at[pl.ds(h * width, width), :], r_o.at[h])
    for slot in range(heads):
        result_of(slot).wait()


def finish(heads, width, rows, out_t, grads, scales, weights, layer_out, new_weights, momentum):
    layer_out[...] = out_t[...].T
    for h in range(heads):
        grad = unpack(grads[h], rows)
        for m in range(3):
            at = (m * heads + h) * width
            part = grad[m * rows : (m + 1) * rows, :]
            momentum[:, at : at + width] = part
            side = LANES // 2 * (m % 2)
            ratio = jnp.concatenate(
                [
                    scales[h, 2 * m : 2 * m + 1, :],
                    scales[h, 2 * m + 1 : 2 * m + 2, :],
                    scales[h, 6 + m // 2 : 7 + m // 2, side : side + LANES // 2],
                ],
                axis=1,
            )
            new_weights[:, at : at + width] = (weights[:, at : at + width] - part) * ratio


def shards(queries, key_vectors, value_vectors, step_sizes, fast_weights, fast_gain, window_gain):
    tokens = queries.shape[0]
    heads = step_sizes.shape[1]
    width = queries.shape[1] // heads
    n = lax.axis_size("seq")
    groups = lax.axis_size("groups")
    group = n // heads
    rows = width // n
    assert tokens == LANES and heads * tokens == WINDOW and group % 2 == 0
    span = heads * LANES
    vmem = pl.BlockSpec(memory_space=pltpu.VMEM)
    hbm = pl.BlockSpec(memory_space=pl.ANY)
    dma = pltpu.SemaphoreType.DMA
    more = max(group - 1, 1)
    token_piece = pltpu.VMEM((heads, width, LANES), BF16)
    level_piece = pltpu.VMEM((heads, 8, LANES), F32)
    assert width == 2 * LANES + LANES // 2
    tall, rest = packing(rows)
    packed = 2 * tall + rest
    loose = max(tall, 2 * rest)
    weight_piece = pltpu.VMEM((heads, packed, LANES), BF16)
    across = pltpu.VMEM((width, span), BF16)
    across_wide = pltpu.VMEM((width, span), F32)
    out_t, grads, scales = pl.pallas_call(
        functools.partial(kernel, n, groups, heads, width),
        out_shape=(
            jax.ShapeDtypeStruct((heads * width, LANES), BF16),
            jax.ShapeDtypeStruct((heads, packed, LANES), BF16),
            jax.ShapeDtypeStruct((heads, 8, LANES), F32),
        ),
        in_specs=[hbm, hbm, hbm, vmem, hbm, vmem, vmem],
        out_specs=(vmem, vmem, vmem),
        scratch_shapes=[
            pltpu.VMEM(queries.shape, BF16),
            pltpu.VMEM(queries.shape, BF16),
            pltpu.VMEM(queries.shape, BF16),
            pltpu.VMEM(fast_weights.shape, F32),
            dma((4,)),
            pltpu.VMEM((heads, 3, width, LANES), BF16),
            weight_piece,
            pltpu.VMEM((heads, loose, width), F32),
            pltpu.VMEM((heads, 2, width, LANES), BF16),
            token_piece,
            token_piece,
            pltpu.VMEM((heads, heads, LANES), F32),
            pltpu.VMEM((n, packed, LANES), BF16),
            pltpu.VMEM((3, width, width), F32),
            pltpu.VMEM((3, width, width), BF16),
            pltpu.VMEM((span, width), BF16),
            across,
            across_wide, across_wide, across, across, across, across,
            pltpu.VMEM((group, heads, loose, width), F32),
            pltpu.VMEM((more, heads, 3 * rows, width), BF16),
            pltpu.VMEM((more, heads, 3 * rows, width), BF16),
            weight_piece,
            pltpu.VMEM((8, width), F32),
            pltpu.VMEM((more, 8, width), F32),
            pltpu.VMEM((8, LANES), F32),
            token_piece,
            pltpu.VMEM((2, width, LANES), F32),
            pltpu.VMEM((heads, width, LANES), F32),
            level_piece,
            pltpu.VMEM((heads, width, LANES), F32),
            token_piece,
            level_piece,
            token_piece,
            level_piece,
            dma((5, heads)), dma((heads,)), dma((heads,)), dma((heads,)), dma((heads,)), dma((heads,)), dma((n,)),
            dma((heads // groups, groups * group)), dma((heads,)),
            dma((heads,)), dma((heads,)), dma((heads,)), dma((heads,)),
            dma((more,)), dma((more,)), dma((more,)), dma((more,)),
            dma((heads,)), dma((heads,)), dma((heads,)), dma((heads,)), dma((heads,)), dma((heads,)),
        ],
        compiler_params=pltpu.CompilerParams(
            collective_id=0, has_side_effects=True, vmem_limit_bytes=60 << 20
        ),
        name="ttt",
    )(key_vectors, value_vectors, queries, step_sizes.T, fast_weights, fast_gain, window_gain)
    return pl.pallas_call(
        functools.partial(finish, heads, width, rows),
        out_shape=(
            jax.ShapeDtypeStruct(queries.shape, BF16),
            jax.ShapeDtypeStruct(fast_weights.shape, F32),
            jax.ShapeDtypeStruct(fast_weights.shape, F32),
        ),
        in_specs=[vmem] * 4,
        out_specs=(vmem, vmem, vmem),
        name="finish",
    )(out_t, grads, scales, fast_weights)


def solution(mesh):
    in_specs = (
        P(("groups", "seq"), None),
        P(("groups", "seq"), None),
        P(("groups", "seq"), None),
        P(("groups", "seq"), None),
        P("seq", None),
        P(),
        P(),
    )
    out_specs = (P(("groups", "seq"), None), P(("groups", "seq"), None), P(("groups", "seq"), None))
    return jax.shard_map(shards, mesh=mesh, in_specs=in_specs, out_specs=out_specs, check_vma=False)
```

```python
import functools
import math

import jax
import jax.numpy as jnp
from jax import lax
from jax.experimental import pallas as pl
from jax.experimental.pallas import tpu as pltpu
from jax.sharding import PartitionSpec as P

WINDOW = 1024
LANES = 128
F32 = jnp.float32
BF16 = jnp.bfloat16


def dot(a, b):
    return jnp.dot(a, b, preferred_element_type=F32)


def dot_nt(a, b):
    return lax.dot_general(a, b, (((1,), (1,)), ((), ())), preferred_element_type=F32)


def dot_tn(a, b):
    return lax.dot_general(a, b, (((0,), (0,)), ((), ())), preferred_element_type=F32)


def packing(rows):
    tall = -(-3 * rows // 16) * 16
    rest = -(-3 * rows // 32) * 16
    return tall, rest


def pack(dst, src, rows):
    tall, rest = packing(rows)
    dst[:tall, :] = src[:tall, :LANES].astype(BF16)
    dst[tall : 2 * tall, :] = src[:tall, LANES : 2 * LANES].astype(BF16)
    sides = [src[:rest, 2 * LANES :], src[rest : 2 * rest, 2 * LANES :]]
    dst[2 * tall :, :] = jnp.concatenate(sides, axis=1).astype(BF16)


def unpack(packed, rows):
    tall, rest = packing(rows)
    packed = packed.astype(F32)
    last = packed[2 * tall :]
    last = jnp.concatenate([last[:, : LANES // 2], last[:, LANES // 2 :]], axis=0)
    return jnp.concatenate([packed[:tall], packed[tall : 2 * tall], last[:tall]], axis=1)


def kernel(
    n, groups, heads, width,
    k_hbm, v_hbm, q_hbm, step_hbm, w_hbm, fast_hbm, window_hbm,
    out, g_out, scale_out,
    k_in, v_in, q_in, weights, step_in, fast_gain, window_gain, s_load,
    kvq_in, w_in, wide,
    kv, qb, qx, stb, wb, wfull, wbf, kn, vt, gates, ups, hid, tgt, gg, gu,
    gstage, gother, ginc, gsend, sums, sinc, scale_send, ostage, gain_cols,
    own_o, own_l, fast_o, xo_stage, xl_stage, xo, xl,
    s_in, r_k, r_v, r_q, r_x, r_st, r_w,
    s_wf, s_xf, s_xo, s_xl, r_xo, r_xl,
    s_gp, r_gp, s_sp, r_sp, s_g, r_g, s_sc, r_sc, s_o, r_o,
):
    group = n // heads
    rows = width // n
    span = heads * LANES
    chunk = 2 * LANES
    chunks = span // chunk
    scale = 1.0 / math.sqrt(width)
    me = lax.axis_index("seq")
    part = lax.axis_index("groups")
    home_block = me // heads
    home_slot = me % heads
    quarter = heads // 2
    spot = me % (2 * heads)
    pair = me // (2 * heads)
    head = spot // 2
    member = 2 * pair + spot % 2
    half = home_block % 2
    local = head // quarter == member % 2

    def place(block, which):
        odd = block % 2
        return (block - odd) * heads + 2 * which + odd

    base = member * heads
    below = member < group - 1
    above = member > 0
    stays = member == home_block

    def remote(src, dst, send, recv, device, to_part=None):
        return pltpu.make_async_remote_copy(
            src_ref=src, dst_ref=dst, send_sem=send, recv_sem=recv,
            device_id={"groups": part if to_part is None else to_part, "seq": device},
            device_id_type=pl.DeviceIdType.MESH,
        )

    loads = [
        pltpu.make_async_copy(src, dst, s_load.at[i])
        for i, (src, dst) in enumerate((
            (w_hbm, weights), (k_hbm, k_in), (v_hbm, v_in), (q_hbm, q_in),
            (step_hbm, step_in), (fast_hbm, fast_gain), (window_hbm, window_gain),
        ))
    ]
    for load in loads:
        load.start()
    barrier = pltpu.get_barrier_semaphore()
    for step in range(1, n):
        pl.semaphore_signal(
            barrier, inc=1, device_id={"seq": lax.rem(me + step, n)},
            device_id_type=pl.DeviceIdType.MESH,
        )
    for other in range(1, groups):
        for d in range(group):
            pl.semaphore_signal(
                barrier, inc=1,
                device_id={"groups": lax.rem(part + other, groups), "seq": place(d, head)},
                device_id_type=pl.DeviceIdType.MESH,
            )

    def flip(m, ref):
        for h in range(0, heads, 2):
            both = ref[:, h * width : (h + 2) * width].T
            kvq_in[h, m] = both[:width]
            kvq_in[h + 1, m] = both[width:]

    loads[0].wait()
    for h in range(heads):
        for m in range(3):
            at = (m * heads + h) * width
            wide[h, m * rows : (m + 1) * rows, :] = weights[:, at : at + width]
        pack(w_in.at[h], wide.at[h], rows)
    loads[1].wait()
    flip(0, k_in)
    pl.semaphore_wait(barrier, n - 1 + (groups - 1) * group)

    def landed(ref, sem):
        pltpu.make_async_copy(ref, ref, sem).wait()

    pending = []

    class Send:
        def __init__(self, src, dst, send, recv, device, local=None, only=None):
            self.ends = (src, dst, recv)
            self.copy = remote(src, dst, send, recv, device)
            self.local, self.only = local, only

        def start(self):
            if self.only is not None:
                pl.when(self.only)(self.copy.start)
            elif self.local is None:
                self.copy.start()
            else:
                pl.when(self.local)(lambda: pltpu.make_async_copy(*self.ends).start())
                pl.when(jnp.logical_not(self.local))(self.copy.start)

        def wait(self):
            if self.only is not None:
                pl.when(self.only)(self.copy.wait_send)
            elif self.local is None:
                self.copy.wait_send()
            else:
                pl.when(jnp.logical_not(self.local))(self.copy.wait_send)

    def spread(src_of, dst, recv, kind):
        sends = []
        for step in range(heads):
            which = lax.rem(head + step, heads)
            sends.append(Send(
                src_of(which), dst, s_in.at[kind, step], recv, place(home_block, which),
                stays if step == 0 else None,
            ))
        return sends

    def feed(after, sends):
        sends = list(sends)
        for done in after:
            done.wait()
            if sends:
                sends.pop(0).start()
        for send in sends:
            send.start()

    stride = heads // groups
    shift = lax.rem(part + 2 * groups * heads - home_slot - head, groups)
    w_sends = []
    for step in range(stride):
        offset = shift + groups * step
        which = lax.rem(head + offset, heads)
        w_sends.append(Send(
            w_in.at[which], wb.at[me], s_in.at[4, step], r_w.at[me], place(home_block, which),
            (offset == 0) & stays if step == 0 else None,
        ))
    feed([], w_sends)
    k_sends = spread(lambda w: kvq_in.at[w, 0], kv.at[home_slot, 0], r_k.at[home_slot], 0)
    feed([], k_sends)
    for load in loads[4:]:
        load.wait()
    loads[2].wait()
    flip(1, v_in)
    v_sends = spread(lambda w: kvq_in.at[w, 1], kv.at[home_slot, 1], r_v.at[home_slot], 1)
    st_sends = spread(lambda w: step_in.at[pl.ds(w, 1), :], stb.at[home_slot], r_st.at[home_slot], 2)
    feed([], v_sends + st_sends)
    loads[3].wait()
    flip(2, q_in)
    q_sends = spread(lambda w: kvq_in.at[w, 2], qb.at[home_slot], r_q.at[home_slot], 3)
    feed([], q_sends)
    first = lax.rem(part + groups * heads - head, groups)

    def share_weights(slot, t, k, to_part, to_member):
        copy = remote(wb.at[slot], wb.at[slot], s_wf.at[t, k], r_w.at[slot], place(to_member, head), to_part)
        copy.start()
        pending.append(copy)

    for t in range(stride):
        slot = base + first + groups * t
        landed(wb.at[slot], r_w.at[slot])
        for d in range(1, group):
            share_weights(slot, t, d, part, lax.rem(member + d, group))
        for other in range(1, groups):
            share_weights(slot, t, other * group, lax.rem(part + other, groups), member)

    for h in range(heads):
        @pl.when(head == h)
        def _():
            at = slice(h * width, (h + 1) * width)
            for m, gain in enumerate((fast_gain, window_gain)):
                gain_cols[m] = jnp.broadcast_to(gain[at].reshape(1, width), (LANES, width)).T

    for d in range(1, group):
        for t in range(stride):
            slot = lax.rem(member + d, group) * heads + first + groups * t
            landed(wb.at[slot], r_w.at[slot])
            for other in range(1, groups):
                share_weights(slot, t, other * group + d, lax.rem(part + other, groups), member)
    key_at = lax.broadcasted_iota(jnp.int32, (span, chunk), 0)
    lane_at = lax.broadcasted_iota(jnp.int32, (1, chunk), 1)

    def soften(scores, values):
        top = jnp.max(scores, axis=0, keepdims=True)
        powers = jnp.exp(scores - top)
        total = jnp.sum(powers, axis=0, keepdims=True)
        probs = (powers * (1.0 / total)).astype(BF16)
        return dot(values, probs), jnp.broadcast_to(top + jnp.log(total), (8, chunk))

    def normalize(field, gain):
        mean_sq = jnp.mean(field * field, axis=0, keepdims=True)
        return field * lax.rsqrt(mean_sq + 1e-05) * gain

    up_there = place(jnp.minimum(member + 1, group - 1), head)
    down_there = place(jnp.maximum(member - 1, 0), head)

    def passed(slot):
        return Send(qb.at[slot], qx.at[slot], s_xf.at[slot], r_x.at[slot], down_there, only=above)

    def raised(slot):
        return (
            remote(xo_stage.at[slot], xo.at[slot], s_xo.at[slot], r_xo.at[slot], up_there),
            remote(xl_stage.at[slot], xl.at[slot], s_xl.at[slot], r_xl.at[slot], up_there),
        )

    def cross(c):
        start = c * chunk
        for slot in (2 * c, 2 * c + 1):
            landed(qx.at[slot], r_x.at[slot])
        query = jnp.concatenate([qx[2 * c], qx[2 * c + 1]], axis=1)
        scores = dot(kn[start:, :], query) * scale
        scores = jnp.where(key_at[start:] > lane_at + start, scores, -1e30)
        field, level = soften(scores, vt[:, start:])
        for half in range(2):
            slot = 2 * c + half
            there = slice(half * LANES, (half + 1) * LANES)
            xo_stage[slot] = field[:, there].astype(BF16)
            xl_stage[slot] = level[:, there]
            for copy in raised(slot):
                copy.start()

    def gate_chunk(c, carry):
        there = pl.ds(pl.multiple_of(c * chunk, chunk), chunk)
        keys = jnp.concatenate([kv[2 * c, 0], kv[2 * c + 1, 0]], axis=1)
        gates[:, there] = dot_tn(wbf[0], keys) * scale
        ups[:, there] = dot_tn(wbf[1], keys) * scale
        return carry

    def grad_chunk(c, carry):
        there = pl.ds(pl.multiple_of(c * chunk, chunk), chunk)
        gate = gates[:, there]
        up = ups[:, there]
        back = dot(wbf[2], tgt[:, there]) * scale
        sigma = jax.nn.sigmoid(gate)
        silu = gate * sigma
        hid[:, there] = (silu * up).astype(BF16)
        gg[:, there] = (back * up * (sigma * (1.0 + gate * (1.0 - sigma)))).astype(BF16)
        gu[:, there] = (back * silu).astype(BF16)
        return carry

    def gother_sends():
        return [
            remote(
                gother.at[d - 1], ginc.at[d - 1], s_gp.at[d - 1], r_gp.at[d - 1],
                place(lax.rem(member + d, group), head),
            )
            for d in range(1, group)
        ]

    def learn():
        for i in range(heads):
            landed(kv.at[i, 0], r_k.at[i])
            kn[i * LANES : (i + 1) * LANES, :] = kv[i, 0].T
        for d in range(group):
            for e in range(1, groups):
                for t in range(stride):
                    slot = lax.rem(member + d, group) * heads + lax.rem(first + e, groups) + groups * t
                    landed(wb.at[slot], r_w.at[slot])
        for s in range(n):
            piece = unpack(wb[s], rows)
            for m in range(3):
                wfull[m, s * rows : (s + 1) * rows, :] = piece[m * rows : (m + 1) * rows, :]
        for m in range(3):
            wbf[m] = wfull[m].astype(BF16)
        lax.fori_loop(0, chunks, gate_chunk, 0)
        for i in range(heads):
            landed(kv.at[i, 1], r_v.at[i])
            landed(stb.at[i], r_st.at[i])
            there = slice(i * LANES, (i + 1) * LANES)
            vt[:, there] = kv[i, 1]
            tgt[:, there] = (-stb[i] * kv[i, 1].astype(F32)).astype(BF16)
        lax.fori_loop(0, chunks, grad_chunk, 0)
        own_keys = jnp.concatenate([kv[i, 0] for i in range(heads)], axis=1)
        for m, (left, right) in enumerate(((own_keys, gg), (own_keys, gu), (hid[...], tgt))):
            grad = dot_nt(left, right[...]) * scale
            for s in range(n):
                gstage[s // heads, s % heads, m * rows : (m + 1) * rows, :] = grad[s * rows : (s + 1) * rows, :]
        for d in range(1, group):
            other = lax.rem(member + d, group)
            for i in range(heads):
                gother[d - 1, i] = gstage[other, i, : 3 * rows, :].astype(BF16)
        for copy in gother_sends():
            copy.start()

    def attend(c):
        reach = (c + 1) * chunk
        query = jnp.concatenate([qb[2 * c], qb[2 * c + 1]], axis=1)
        scores = dot(kn[:reach, :], query) * scale
        scores = jnp.where(key_at[:reach] <= lane_at + c * chunk, scores, -1e30)
        attended, level = soften(scores, vt[:, :reach])
        gate = dot_tn(wbf[0], query) * scale
        up = dot_tn(wbf[1], query) * scale
        hidden = (gate * jax.nn.sigmoid(gate) * up).astype(BF16)
        fast = dot_tn(wbf[2], hidden) * scale
        for half in range(2):
            there = slice(half * LANES, (half + 1) * LANES)
            own_o[2 * c + half] = attended[:, there]
            own_l[2 * c + half] = level[:, there]
            fast_o[2 * c + half] = normalize(fast[:, there], gain_cols[0])

    def result_of(slot):
        dst = out.at[pl.ds(pl.multiple_of(head * width, 64), width), :]
        return Send(ostage.at[slot], dst, s_o.at[slot], r_o.at[head], base + slot, base + slot == me)

    def finalize(slot):
        @pl.when(above)
        def _():
            landed(xo.at[slot], r_xo.at[slot])
            landed(xl.at[slot], r_xl.at[slot])
            here = own_l[slot, 0:1, :]
            there = xl[slot, 0:1, :]
            share = 1.0 / (1.0 + jnp.exp(there - here))
            rest = 1.0 / (1.0 + jnp.exp(here - there))
            own_o[slot] = own_o[slot] * share + xo[slot].astype(F32) * rest

        ostage[slot] = (fast_o[slot] + normalize(own_o[slot], gain_cols[1])).astype(BF16)
        result_of(slot).start()

    def g_sends(src_of, dst, send, recv):
        sends = []
        for step in range(heads):
            i = lax.rem(home_slot + step, heads)
            sends.append(Send(src_of(i), dst.at[head], send.at[step], recv.at[head], base + i, stays if step == 0 else None))
        return sends

    def partner_sums():
        return [
            remote(sums, sinc.at[d - 1], s_sp.at[d - 1], r_sp.at[d - 1], place(lax.rem(member + d, group), head))
            for d in range(1, group)
        ]

    def gather_gradient():
        for d in range(1, group):
            landed(ginc.at[d - 1], r_gp.at[d - 1])
        sums[...] = jnp.zeros_like(sums)

        def add_up(i, carry):
            total = gstage[member, i, : 3 * rows, :]
            for d in range(1, group):
                total = total + ginc[d - 1, i].astype(F32)
            gstage[member, i, : 3 * rows, :] = total
            pack(gsend.at[i], gstage.at[member, i], rows)
            weight = unpack(wb[base + i], rows)[: 3 * rows]
            moved = weight - total
            for m in range(3):
                piece = slice(m * rows, (m + 1) * rows)
                old = weight[piece, :]
                new = moved[piece, :]
                sums[m : m + 1, :] += jnp.sum(old * old, axis=0, keepdims=True)
                sums[4 + m : 5 + m, :] += jnp.sum(new * new, axis=0, keepdims=True)
            return carry

        lax.fori_loop(0, heads, add_up, 0)
        for copy in partner_sums():
            copy.start()
        for send in g_sends(lambda i: gsend.at[i], g_out, s_g, r_g):
            send.start()

    def send_scales():
        for d in range(1, group):
            landed(sinc.at[d - 1], r_sp.at[d - 1])
        total = sums[...]
        for d in range(1, group):
            total = total + sinc[d - 1]
        ratio = jnp.sqrt((total[0:4] + 1e-06) / (total[4:8] + 1e-06))
        for m in range(3):
            scale_send[2 * m : 2 * m + 1, :] = ratio[m : m + 1, :LANES]
            scale_send[2 * m + 1 : 2 * m + 2, :] = ratio[m : m + 1, LANES : 2 * LANES]
        scale_send[6:7, :] = jnp.concatenate([ratio[0:1, 2 * LANES :], ratio[1:2, 2 * LANES :]], axis=1)
        scale_send[7:8, :] = jnp.concatenate([ratio[2:3, 2 * LANES :], ratio[2:3, 2 * LANES :]], axis=1)
        for send in g_sends(lambda i: scale_send, scale_out, s_sc, r_sc):
            send.start()

    turn = head % chunks

    def each_chunk(act):
        def body(t, carry):
            act(lax.rem(turn + t, chunks))
            return carry

        lax.fori_loop(0, chunks, body, 0)

    def choose(act, now):
        for c in range(chunks):
            pl.when(now == c)(functools.partial(act, c))

    def finish_chunk(now):
        finalize(2 * now)
        finalize(2 * now + 1)

    def attend_chunk(now):
        choose(attend, now)
        pl.when(jnp.logical_not(local & above))(lambda: finish_chunk(now))

    def attend_all():
        for t in range(heads):
            slot = lax.rem(2 * turn + t, heads)
            landed(qb.at[slot], r_q.at[slot])
            passed(slot).start()
        each_chunk(attend_chunk)

    def cross_all():
        each_chunk(lambda now: choose(cross, now))

    learn()
    gather_gradient()
    send_scales()
    pl.when(below & jnp.logical_not(local))(cross_all)
    attend_all()
    pl.when(below & local)(cross_all)

    @pl.when(local & above)
    def _():
        each_chunk(finish_chunk)

    for copy in pending:
        copy.wait_send()
    for send in w_sends + st_sends + k_sends + v_sends + q_sends:
        send.wait()
    for send in g_sends(lambda i: gsend.at[i], g_out, s_g, r_g) + g_sends(lambda i: scale_send, scale_out, s_sc, r_sc):
        send.wait()
    for copy in partner_sums() + gother_sends():
        copy.wait_send()
    for slot in range(heads):
        passed(slot).wait()

    @pl.when(below)
    def _():
        for slot in range(heads):
            for copy in raised(slot):
                copy.wait_send()

    for h in range(heads):
        landed(g_out.at[h], r_g.at[h])
        landed(scale_out.at[h], r_sc.at[h])
        landed(out.at[pl.ds(h * width, width), :], r_o.at[h])
    for slot in range(heads):
        result_of(slot).wait()


def finish(heads, width, rows, out_t, grads, scales, weights, layer_out, new_weights, momentum):
    layer_out[...] = out_t[...].T
    for h in range(heads):
        grad = unpack(grads[h], rows)
        for m in range(3):
            at = (m * heads + h) * width
            part = grad[m * rows : (m + 1) * rows, :]
            momentum[:, at : at + width] = part
            side = LANES // 2 * (m % 2)
            ratio = jnp.concatenate(
                [
                    scales[h, 2 * m : 2 * m + 1, :],
                    scales[h, 2 * m + 1 : 2 * m + 2, :],
                    scales[h, 6 + m // 2 : 7 + m // 2, side : side + LANES // 2],
                ],
                axis=1,
            )
            new_weights[:, at : at + width] = (weights[:, at : at + width] - part) * ratio


def shards(queries, key_vectors, value_vectors, step_sizes, fast_weights, fast_gain, window_gain):
    tokens = queries.shape[0]
    heads = step_sizes.shape[1]
    width = queries.shape[1] // heads
    n = lax.axis_size("seq")
    groups = lax.axis_size("groups")
    group = n // heads
    rows = width // n
    assert tokens == LANES and heads * tokens == WINDOW and group % 2 == 0
    span = heads * LANES
    vmem = pl.BlockSpec(memory_space=pltpu.VMEM)
    hbm = pl.BlockSpec(memory_space=pltpu.HBM)
    dma = pltpu.SemaphoreType.DMA
    more = max(group - 1, 1)
    token_piece = pltpu.VMEM((heads, width, LANES), BF16)
    level_piece = pltpu.VMEM((heads, 8, LANES), F32)
    assert width == 2 * LANES + LANES // 2
    tall, rest = packing(rows)
    packed = 2 * tall + rest
    loose = max(tall, 2 * rest)
    weight_piece = pltpu.VMEM((heads, packed, LANES), BF16)
    across = pltpu.VMEM((width, span), BF16)
    across_wide = pltpu.VMEM((width, span), F32)
    out_t, grads, scales = pl.pallas_call(
        functools.partial(kernel, n, groups, heads, width),
        out_shape=(
            jax.ShapeDtypeStruct((heads * width, LANES), BF16),
            jax.ShapeDtypeStruct((heads, packed, LANES), BF16),
            jax.ShapeDtypeStruct((heads, 8, LANES), F32),
        ),
        in_specs=[hbm] * 7,
        out_specs=(vmem, vmem, vmem),
        scratch_shapes=[
            pltpu.VMEM(queries.shape, BF16),
            pltpu.VMEM(queries.shape, BF16),
            pltpu.VMEM(queries.shape, BF16),
            pltpu.VMEM(fast_weights.shape, F32),
            pltpu.VMEM(step_sizes.shape[::-1], F32),
            pltpu.VMEM(fast_gain.shape, F32),
            pltpu.VMEM(window_gain.shape, F32),
            dma((7,)),
            pltpu.VMEM((heads, 3, width, LANES), BF16),
            weight_piece,
            pltpu.VMEM((heads, loose, width), F32),
            pltpu.VMEM((heads, 2, width, LANES), BF16),
            token_piece,
            token_piece,
            pltpu.VMEM((heads, 1, LANES), F32),
            pltpu.VMEM((n, packed, LANES), BF16),
            pltpu.VMEM((3, width, width), F32),
            pltpu.VMEM((3, width, width), BF16),
            pltpu.VMEM((span, width), BF16),
            across,
            across_wide, across_wide, across, across, across, across,
            pltpu.VMEM((group, heads, loose, width), F32),
            pltpu.VMEM((more, heads, 3 * rows, width), BF16),
            pltpu.VMEM((more, heads, 3 * rows, width), BF16),
            weight_piece,
            pltpu.VMEM((8, width), F32),
            pltpu.VMEM((more, 8, width), F32),
            pltpu.VMEM((8, LANES), F32),
            token_piece,
            pltpu.VMEM((2, width, LANES), F32),
            pltpu.VMEM((heads, width, LANES), F32),
            level_piece,
            pltpu.VMEM((heads, width, LANES), F32),
            token_piece,
            level_piece,
            token_piece,
            level_piece,
            dma((5, heads)), dma((heads,)), dma((heads,)), dma((heads,)), dma((heads,)), dma((heads,)), dma((n,)),
            dma((heads // groups, groups * group)), dma((heads,)),
            dma((heads,)), dma((heads,)), dma((heads,)), dma((heads,)),
            dma((more,)), dma((more,)), dma((more,)), dma((more,)),
            dma((heads,)), dma((heads,)), dma((heads,)), dma((heads,)), dma((heads,)), dma((heads,)),
        ],
        compiler_params=pltpu.CompilerParams(
            collective_id=0, has_side_effects=True, vmem_limit_bytes=40 << 20
        ),
        name="ttt",
    )(*[pltpu.with_memory_space_constraint(a, pltpu.HBM) for a in (
        key_vectors, value_vectors, queries, step_sizes.T, fast_weights, fast_gain, window_gain
    )])
    return pl.pallas_call(
        functools.partial(finish, heads, width, rows),
        out_shape=(
            jax.ShapeDtypeStruct(queries.shape, BF16),
            jax.ShapeDtypeStruct(fast_weights.shape, F32),
            jax.ShapeDtypeStruct(fast_weights.shape, F32),
        ),
        in_specs=[vmem] * 4,
        out_specs=(vmem, vmem, vmem),
        compiler_params=pltpu.CompilerParams(vmem_limit_bytes=12 << 20),
        name="finish",
    )(out_t, grads, scales, fast_weights)


def solution(mesh):
    in_specs = (
        P(("groups", "seq"), None),
        P(("groups", "seq"), None),
        P(("groups", "seq"), None),
        P(("groups", "seq"), None),
        P("seq", None),
        P(),
        P(),
    )
    out_specs = (P(("groups", "seq"), None), P(("groups", "seq"), None), P(("groups", "seq"), None))
    return jax.shard_map(shards, mesh=mesh, in_specs=in_specs, out_specs=out_specs, check_vma=False)
```

```python
import functools
import math

import jax
import jax.numpy as jnp
from jax import lax
from jax.experimental import pallas as pl
from jax.experimental.pallas import tpu as pltpu
from jax.sharding import PartitionSpec as P

WINDOW = 1024
LANES = 128
F32 = jnp.float32
BF16 = jnp.bfloat16


def dot(a, b):
    return jnp.dot(a, b, preferred_element_type=F32)


def dot_nt(a, b):
    return lax.dot_general(a, b, (((1,), (1,)), ((), ())), preferred_element_type=F32)


def dot_tn(a, b):
    return lax.dot_general(a, b, (((0,), (0,)), ((), ())), preferred_element_type=F32)


def packing(rows):
    tall = -(-3 * rows // 16) * 16
    rest = -(-3 * rows // 32) * 16
    return tall, rest


def pack(dst, src, rows):
    tall, rest = packing(rows)
    dst[:tall, :] = src[:tall, :LANES].astype(BF16)
    dst[tall : 2 * tall, :] = src[:tall, LANES : 2 * LANES].astype(BF16)
    sides = [src[:rest, 2 * LANES :], src[rest : 2 * rest, 2 * LANES :]]
    dst[2 * tall :, :] = jnp.concatenate(sides, axis=1).astype(BF16)


def unpack(packed, rows):
    tall, rest = packing(rows)
    packed = packed.astype(F32)
    last = packed[2 * tall :]
    last = jnp.concatenate([last[:, : LANES // 2], last[:, LANES // 2 :]], axis=0)
    return jnp.concatenate([packed[:tall], packed[tall : 2 * tall], last[:tall]], axis=1)


def kernel(
    n, groups, heads, width,
    k_hbm, v_hbm, q_hbm, step_hbm, w_hbm, fast_hbm, window_hbm,
    layer_out, new_weights, momentum,
    out, g_out, scale_out,
    k_in, v_in, q_in, weights, step_in, fast_gain, window_gain, s_load,
    kvq_in, w_in, wide,
    kv, qb, qx, stb, wb, wfull, wbf, kn, vt, gates, ups, hid, tgt, gg, gu,
    gstage, gother, ginc, gsend, sums, sinc, scale_send, ostage, gain_cols,
    own_o, own_l, fast_o, xo_stage, xl_stage, xo, xl,
    s_in, r_k, r_v, r_q, r_x, r_st, r_w,
    s_wf, s_xf, s_xo, s_xl, r_xo, r_xl,
    s_gp, r_gp, s_sp, r_sp, s_g, r_g, s_sc, r_sc, s_o, r_o,
):
    group = n // heads
    rows = width // n
    span = heads * LANES
    chunk = 2 * LANES
    chunks = span // chunk
    scale = 1.0 / math.sqrt(width)
    me = lax.axis_index("seq")
    part = lax.axis_index("groups")
    home_block = me // heads
    home_slot = me % heads
    quarter = heads // 2
    spot = me % (2 * heads)
    pair = me // (2 * heads)
    head = spot // 2
    member = 2 * pair + spot % 2
    half = home_block % 2
    local = head // quarter == member % 2

    def place(block, which):
        odd = block % 2
        return (block - odd) * heads + 2 * which + odd

    base = member * heads
    below = member < group - 1
    above = member > 0
    stays = member == home_block

    def remote(src, dst, send, recv, device, to_part=None):
        return pltpu.make_async_remote_copy(
            src_ref=src, dst_ref=dst, send_sem=send, recv_sem=recv,
            device_id={"groups": part if to_part is None else to_part, "seq": device},
            device_id_type=pl.DeviceIdType.MESH,
        )

    loads = [
        pltpu.make_async_copy(src, dst, s_load.at[i])
        for i, (src, dst) in enumerate((
            (w_hbm, weights), (k_hbm, k_in), (v_hbm, v_in), (q_hbm, q_in),
            (step_hbm, step_in), (fast_hbm, fast_gain), (window_hbm, window_gain),
        ))
    ]
    for load in loads:
        load.start()
    barrier = pltpu.get_barrier_semaphore()
    for step in range(1, n):
        pl.semaphore_signal(
            barrier, inc=1, device_id={"seq": lax.rem(me + step, n)},
            device_id_type=pl.DeviceIdType.MESH,
        )
    for other in range(1, groups):
        for d in range(group):
            pl.semaphore_signal(
                barrier, inc=1,
                device_id={"groups": lax.rem(part + other, groups), "seq": place(d, head)},
                device_id_type=pl.DeviceIdType.MESH,
            )

    def flip(m, ref):
        for h in range(0, heads, 2):
            both = ref[:, h * width : (h + 2) * width].T
            kvq_in[h, m] = both[:width]
            kvq_in[h + 1, m] = both[width:]

    loads[0].wait()
    for h in range(heads):
        for m in range(3):
            at = (m * heads + h) * width
            wide[h, m * rows : (m + 1) * rows, :] = weights[:, at : at + width]
        pack(w_in.at[h], wide.at[h], rows)
    loads[1].wait()
    flip(0, k_in)
    loads[2].wait()
    flip(1, v_in)
    pl.semaphore_wait(barrier, n - 1 + (groups - 1) * group)

    def landed(ref, sem):
        pltpu.make_async_copy(ref, ref, sem).wait()

    pending = []

    class Send:
        def __init__(self, src, dst, send, recv, device, local=None, only=None):
            self.ends = (src, dst, recv)
            self.copy = remote(src, dst, send, recv, device)
            self.local, self.only = local, only

        def start(self):
            if self.only is not None:
                pl.when(self.only)(self.copy.start)
            elif self.local is None:
                self.copy.start()
            else:
                pl.when(self.local)(lambda: pltpu.make_async_copy(*self.ends).start())
                pl.when(jnp.logical_not(self.local))(self.copy.start)

        def wait(self):
            if self.only is not None:
                pl.when(self.only)(self.copy.wait_send)
            elif self.local is None:
                self.copy.wait_send()
            else:
                pl.when(jnp.logical_not(self.local))(self.copy.wait_send)

    def spread(src_of, dst, recv, kind):
        sends = []
        for step in range(heads):
            which = lax.rem(head + step, heads)
            sends.append(Send(
                src_of(which), dst, s_in.at[kind, step], recv, place(home_block, which),
                stays if step == 0 else None,
            ))
        return sends

    def feed(after, sends):
        sends = list(sends)
        for done in after:
            done.wait()
            if sends:
                sends.pop(0).start()
        for send in sends:
            send.start()

    stride = heads // groups
    shift = lax.rem(part + 2 * groups * heads - home_slot - head, groups)
    w_sends = []
    for step in range(stride):
        offset = shift + groups * step
        which = lax.rem(head + offset, heads)
        w_sends.append(Send(
            w_in.at[which], wb.at[me], s_in.at[4, step], r_w.at[me], place(home_block, which),
            (offset == 0) & stays if step == 0 else None,
        ))
    feed([], w_sends)
    k_sends = spread(lambda w: kvq_in.at[w, 0], kv.at[home_slot, 0], r_k.at[home_slot], 0)
    feed([], k_sends)
    for load in loads[4:]:
        load.wait()
    v_sends = spread(lambda w: kvq_in.at[w, 1], kv.at[home_slot, 1], r_v.at[home_slot], 1)
    st_sends = spread(lambda w: step_in.at[pl.ds(w, 1), :], stb.at[home_slot], r_st.at[home_slot], 2)
    feed([], v_sends + st_sends)
    loads[3].wait()
    flip(2, q_in)
    q_sends = spread(lambda w: kvq_in.at[w, 2], qb.at[home_slot], r_q.at[home_slot], 3)
    feed([], q_sends)
    first = lax.rem(part + groups * heads - head, groups)

    def share_weights(slot, t, k, to_part, to_member):
        copy = remote(wb.at[slot], wb.at[slot], s_wf.at[t, k], r_w.at[slot], place(to_member, head), to_part)
        copy.start()
        pending.append(copy)

    for t in range(stride):
        slot = base + first + groups * t
        landed(wb.at[slot], r_w.at[slot])
        for d in range(1, group):
            share_weights(slot, t, d, part, lax.rem(member + d, group))
        for other in range(1, groups):
            share_weights(slot, t, other * group, lax.rem(part + other, groups), member)

    for h in range(heads):
        @pl.when(head == h)
        def _():
            at = slice(h * width, (h + 1) * width)
            for m, gain in enumerate((fast_gain, window_gain)):
                gain_cols[m] = jnp.broadcast_to(gain[at].reshape(1, width), (LANES, width)).T

    for d in range(1, group):
        for t in range(stride):
            slot = lax.rem(member + d, group) * heads + first + groups * t
            landed(wb.at[slot], r_w.at[slot])
            for other in range(1, groups):
                share_weights(slot, t, other * group + d, lax.rem(part + other, groups), member)
    key_at = lax.broadcasted_iota(jnp.int32, (span, chunk), 0)
    lane_at = lax.broadcasted_iota(jnp.int32, (1, chunk), 1)

    def soften(scores, values):
        top = jnp.max(scores, axis=0, keepdims=True)
        powers = jnp.exp(scores - top)
        total = jnp.sum(powers, axis=0, keepdims=True)
        probs = (powers * (1.0 / total)).astype(BF16)
        return dot(values, probs), jnp.broadcast_to(top + jnp.log(total), (8, chunk))

    def normalize(field, gain):
        mean_sq = jnp.mean(field * field, axis=0, keepdims=True)
        return field * lax.rsqrt(mean_sq + 1e-05) * gain

    up_there = place(jnp.minimum(member + 1, group - 1), head)
    down_there = place(jnp.maximum(member - 1, 0), head)

    def passed(slot):
        return Send(qb.at[slot], qx.at[slot], s_xf.at[slot], r_x.at[slot], down_there, only=above)

    def raised(slot):
        return (
            remote(xo_stage.at[slot], xo.at[slot], s_xo.at[slot], r_xo.at[slot], up_there),
            remote(xl_stage.at[slot], xl.at[slot], s_xl.at[slot], r_xl.at[slot], up_there),
        )

    def cross(c):
        start = c * chunk
        for slot in (2 * c, 2 * c + 1):
            landed(qx.at[slot], r_x.at[slot])
        query = jnp.concatenate([qx[2 * c], qx[2 * c + 1]], axis=1)
        scores = dot(kn[start:, :], query) * scale
        scores = jnp.where(key_at[start:] > lane_at + start, scores, -1e30)
        field, level = soften(scores, vt[:, start:])
        for half in range(2):
            slot = 2 * c + half
            there = slice(half * LANES, (half + 1) * LANES)
            xo_stage[slot] = field[:, there].astype(BF16)
            xl_stage[slot] = level[:, there]
            for copy in raised(slot):
                copy.start()

    def gate_chunk(c, carry):
        there = pl.ds(pl.multiple_of(c * chunk, chunk), chunk)
        keys = jnp.concatenate([kv[2 * c, 0], kv[2 * c + 1, 0]], axis=1)
        gates[:, there] = dot_tn(wbf[0], keys) * scale
        ups[:, there] = dot_tn(wbf[1], keys) * scale
        return carry

    def grad_chunk(c, carry):
        there = pl.ds(pl.multiple_of(c * chunk, chunk), chunk)
        gate = gates[:, there]
        up = ups[:, there]
        back = dot(wbf[2], tgt[:, there]) * scale
        sigma = jax.nn.sigmoid(gate)
        silu = gate * sigma
        hid[:, there] = (silu * up).astype(BF16)
        gg[:, there] = (back * up * (sigma * (1.0 + gate * (1.0 - sigma)))).astype(BF16)
        gu[:, there] = (back * silu).astype(BF16)
        return carry

    def gother_sends():
        return [
            remote(
                gother.at[d - 1], ginc.at[d - 1], s_gp.at[d - 1], r_gp.at[d - 1],
                place(lax.rem(member + d, group), head),
            )
            for d in range(1, group)
        ]

    def learn():
        for i in range(heads):
            landed(kv.at[i, 0], r_k.at[i])
            kn[i * LANES : (i + 1) * LANES, :] = kv[i, 0].T
        for d in range(group):
            for e in range(1, groups):
                for t in range(stride):
                    slot = lax.rem(member + d, group) * heads + lax.rem(first + e, groups) + groups * t
                    landed(wb.at[slot], r_w.at[slot])
        for s in range(n):
            piece = unpack(wb[s], rows)
            for m in range(3):
                wfull[m, s * rows : (s + 1) * rows, :] = piece[m * rows : (m + 1) * rows, :]
        for m in range(3):
            wbf[m] = wfull[m].astype(BF16)
        lax.fori_loop(0, chunks, gate_chunk, 0)
        for i in range(heads):
            landed(kv.at[i, 1], r_v.at[i])
            landed(stb.at[i], r_st.at[i])
            there = slice(i * LANES, (i + 1) * LANES)
            vt[:, there] = kv[i, 1]
            tgt[:, there] = (-stb[i] * kv[i, 1].astype(F32)).astype(BF16)
        lax.fori_loop(0, chunks, grad_chunk, 0)
        own_keys = jnp.concatenate([kv[i, 0] for i in range(heads)], axis=1)
        for m, (left, right) in enumerate(((own_keys, gg), (own_keys, gu), (hid[...], tgt))):
            grad = dot_nt(left, right[...]) * scale
            for s in range(n):
                gstage[s // heads, s % heads, m * rows : (m + 1) * rows, :] = grad[s * rows : (s + 1) * rows, :]
        for d in range(1, group):
            other = lax.rem(member + d, group)
            for i in range(heads):
                gother[d - 1, i] = gstage[other, i, : 3 * rows, :].astype(BF16)
        for copy in gother_sends():
            copy.start()

    def attend(c):
        reach = (c + 1) * chunk
        query = jnp.concatenate([qb[2 * c], qb[2 * c + 1]], axis=1)
        scores = dot(kn[:reach, :], query) * scale
        scores = jnp.where(key_at[:reach] <= lane_at + c * chunk, scores, -1e30)
        attended, level = soften(scores, vt[:, :reach])
        gate = dot_tn(wbf[0], query) * scale
        up = dot_tn(wbf[1], query) * scale
        hidden = (gate * jax.nn.sigmoid(gate) * up).astype(BF16)
        fast = dot_tn(wbf[2], hidden) * scale
        for half in range(2):
            there = slice(half * LANES, (half + 1) * LANES)
            own_o[2 * c + half] = attended[:, there]
            own_l[2 * c + half] = level[:, there]
            fast_o[2 * c + half] = normalize(fast[:, there], gain_cols[0])

    def result_of(slot):
        dst = out.at[pl.ds(pl.multiple_of(head * width, 64), width), :]
        return Send(ostage.at[slot], dst, s_o.at[slot], r_o.at[head], base + slot, base + slot == me)

    def finalize(slot):
        @pl.when(above)
        def _():
            landed(xo.at[slot], r_xo.at[slot])
            landed(xl.at[slot], r_xl.at[slot])
            here = own_l[slot, 0:1, :]
            there = xl[slot, 0:1, :]
            share = 1.0 / (1.0 + jnp.exp(there - here))
            rest = 1.0 / (1.0 + jnp.exp(here - there))
            own_o[slot] = own_o[slot] * share + xo[slot].astype(F32) * rest

        ostage[slot] = (fast_o[slot] + normalize(own_o[slot], gain_cols[1])).astype(BF16)
        result_of(slot).start()

    def g_sends(src_of, dst, send, recv):
        sends = []
        for step in range(heads):
            i = lax.rem(home_slot + step, heads)
            sends.append(Send(src_of(i), dst.at[head], send.at[step], recv.at[head], base + i, stays if step == 0 else None))
        return sends

    def partner_sums():
        return [
            remote(sums, sinc.at[d - 1], s_sp.at[d - 1], r_sp.at[d - 1], place(lax.rem(member + d, group), head))
            for d in range(1, group)
        ]

    def gather_gradient():
        for d in range(1, group):
            landed(ginc.at[d - 1], r_gp.at[d - 1])
        sums[...] = jnp.zeros_like(sums)

        def add_up(i, carry):
            total = gstage[member, i, : 3 * rows, :]
            for d in range(1, group):
                total = total + ginc[d - 1, i].astype(F32)
            gstage[member, i, : 3 * rows, :] = total
            pack(gsend.at[i], gstage.at[member, i], rows)
            weight = unpack(wb[base + i], rows)[: 3 * rows]
            moved = weight - total
            for m in range(3):
                piece = slice(m * rows, (m + 1) * rows)
                old = weight[piece, :]
                new = moved[piece, :]
                sums[m : m + 1, :] += jnp.sum(old * old, axis=0, keepdims=True)
                sums[4 + m : 5 + m, :] += jnp.sum(new * new, axis=0, keepdims=True)
            return carry

        lax.fori_loop(0, heads, add_up, 0)
        for copy in partner_sums():
            copy.start()
        for send in g_sends(lambda i: gsend.at[i], g_out, s_g, r_g):
            send.start()

    def send_scales():
        for d in range(1, group):
            landed(sinc.at[d - 1], r_sp.at[d - 1])
        total = sums[...]
        for d in range(1, group):
            total = total + sinc[d - 1]
        ratio = jnp.sqrt((total[0:4] + 1e-06) / (total[4:8] + 1e-06))
        for m in range(3):
            scale_send[2 * m : 2 * m + 1, :] = ratio[m : m + 1, :LANES]
            scale_send[2 * m + 1 : 2 * m + 2, :] = ratio[m : m + 1, LANES : 2 * LANES]
        scale_send[6:7, :] = jnp.concatenate([ratio[0:1, 2 * LANES :], ratio[1:2, 2 * LANES :]], axis=1)
        scale_send[7:8, :] = jnp.concatenate([ratio[2:3, 2 * LANES :], ratio[2:3, 2 * LANES :]], axis=1)
        for send in g_sends(lambda i: scale_send, scale_out, s_sc, r_sc):
            send.start()

    turn = head % chunks

    def each_chunk(act):
        def body(t, carry):
            act(lax.rem(turn + chunks - t, chunks))
            return carry

        lax.fori_loop(0, chunks, body, 0)

    def choose(act, now):
        for c in range(chunks):
            pl.when(now == c)(functools.partial(act, c))

    def finish_chunk(now):
        finalize(2 * now)
        finalize(2 * now + 1)

    def attend_chunk(now):
        for slot in (2 * now, 2 * now + 1):
            landed(qb.at[slot], r_q.at[slot])
            passed(slot).start()
        choose(attend, now)
        pl.when(jnp.logical_not(local & above))(lambda: finish_chunk(now))

    def attend_all():
        each_chunk(attend_chunk)

    def cross_all():
        each_chunk(lambda now: choose(cross, now))

    learn()
    gather_gradient()
    send_scales()
    pl.when(below & jnp.logical_not(local))(cross_all)
    attend_all()
    pl.when(below & local)(cross_all)

    @pl.when(local & above)
    def _():
        each_chunk(finish_chunk)

    for h in range(heads):
        landed(g_out.at[h], r_g.at[h])
        landed(scale_out.at[h], r_sc.at[h])
        grad = unpack(g_out[h], rows)
        for m in range(3):
            at = (m * heads + h) * width
            piece = grad[m * rows : (m + 1) * rows, :]
            side = LANES // 2 * (m % 2)
            ratio = jnp.concatenate(
                [
                    scale_out[h, 2 * m : 2 * m + 1, :],
                    scale_out[h, 2 * m + 1 : 2 * m + 2, :],
                    scale_out[h, 6 + m // 2 : 7 + m // 2, side : side + LANES // 2],
                ],
                axis=1,
            )
            momentum[:, at : at + width] = piece
            new_weights[:, at : at + width] = (weights[:, at : at + width] - piece) * ratio
    for copy in pending:
        copy.wait_send()
    for send in w_sends + st_sends + k_sends + v_sends + q_sends:
        send.wait()
    for send in g_sends(lambda i: gsend.at[i], g_out, s_g, r_g) + g_sends(lambda i: scale_send, scale_out, s_sc, r_sc):
        send.wait()
    for copy in partner_sums() + gother_sends():
        copy.wait_send()
    for slot in range(heads):
        passed(slot).wait()

    @pl.when(below)
    def _():
        for slot in range(heads):
            for copy in raised(slot):
                copy.wait_send()

    for h in range(0, heads, 2):
        for i in (h, h + 1):
            landed(out.at[pl.ds(i * width, width), :], r_o.at[i])
        at = slice(h * width, (h + 2) * width)
        layer_out[:, at] = out[at, :].T
    for slot in range(heads):
        result_of(slot).wait()


def finish(a, b, c, x, y, z, sems):
    copies = [pltpu.make_async_copy(*ends, sems.at[i]) for i, ends in enumerate(((a, x), (b, y), (c, z)))]
    for copy in copies:
        copy.start()
    for copy in copies:
        copy.wait()


def shards(queries, key_vectors, value_vectors, step_sizes, fast_weights, fast_gain, window_gain):
    tokens = queries.shape[0]
    heads = step_sizes.shape[1]
    width = queries.shape[1] // heads
    n = lax.axis_size("seq")
    groups = lax.axis_size("groups")
    group = n // heads
    rows = width // n
    assert tokens == LANES and heads * tokens == WINDOW and group % 2 == 0
    span = heads * LANES
    vmem = pl.BlockSpec(memory_space=pltpu.VMEM)
    hbm = pl.BlockSpec(memory_space=pl.ANY)
    dma = pltpu.SemaphoreType.DMA
    more = max(group - 1, 1)
    token_piece = pltpu.VMEM((heads, width, LANES), BF16)
    level_piece = pltpu.VMEM((heads, 8, LANES), F32)
    assert width == 2 * LANES + LANES // 2
    tall, rest = packing(rows)
    packed = 2 * tall + rest
    loose = max(tall, 2 * rest)
    weight_piece = pltpu.VMEM((heads, packed, LANES), BF16)
    across = pltpu.VMEM((width, span), BF16)
    across_wide = pltpu.VMEM((width, span), F32)
    results = pl.pallas_call(
        functools.partial(kernel, n, groups, heads, width),
        out_shape=(
            jax.ShapeDtypeStruct(queries.shape, BF16),
            jax.ShapeDtypeStruct(fast_weights.shape, F32),
            jax.ShapeDtypeStruct(fast_weights.shape, F32),
        ),
        in_specs=[hbm] * 7,
        out_specs=(vmem, vmem, vmem),
        scratch_shapes=[
            pltpu.VMEM((heads * width, LANES), BF16),
            weight_piece,
            pltpu.VMEM((heads, 8, LANES), F32),
            pltpu.VMEM(queries.shape, BF16),
            pltpu.VMEM(queries.shape, BF16),
            pltpu.VMEM(queries.shape, BF16),
            pltpu.VMEM(fast_weights.shape, F32),
            pltpu.VMEM(step_sizes.shape[::-1], F32),
            pltpu.VMEM(fast_gain.shape, F32),
            pltpu.VMEM(window_gain.shape, F32),
            dma((7,)),
            pltpu.VMEM((heads, 3, width, LANES), BF16),
            weight_piece,
            pltpu.VMEM((heads, loose, width), F32),
            pltpu.VMEM((heads, 2, width, LANES), BF16),
            token_piece,
            token_piece,
            pltpu.VMEM((heads, 1, LANES), F32),
            pltpu.VMEM((n, packed, LANES), BF16),
            pltpu.VMEM((3, width, width), F32),
            pltpu.VMEM((3, width, width), BF16),
            pltpu.VMEM((span, width), BF16),
            across,
            across_wide, across_wide, across, across, across, across,
            pltpu.VMEM((group, heads, loose, width), F32),
            pltpu.VMEM((more, heads, 3 * rows, width), BF16),
            pltpu.VMEM((more, heads, 3 * rows, width), BF16),
            weight_piece,
            pltpu.VMEM((8, width), F32),
            pltpu.VMEM((more, 8, width), F32),
            pltpu.VMEM((8, LANES), F32),
            token_piece,
            pltpu.VMEM((2, width, LANES), F32),
            pltpu.VMEM((heads, width, LANES), F32),
            level_piece,
            pltpu.VMEM((heads, width, LANES), F32),
            token_piece,
            level_piece,
            token_piece,
            level_piece,
            dma((5, heads)), dma((heads,)), dma((heads,)), dma((heads,)), dma((heads,)), dma((heads,)), dma((n,)),
            dma((heads // groups, groups * group)), dma((heads,)),
            dma((heads,)), dma((heads,)), dma((heads,)), dma((heads,)),
            dma((more,)), dma((more,)), dma((more,)), dma((more,)),
            dma((heads,)), dma((heads,)), dma((heads,)), dma((heads,)), dma((heads,)), dma((heads,)),
        ],
        compiler_params=pltpu.CompilerParams(
            collective_id=0, has_side_effects=True, vmem_limit_bytes=40 << 20
        ),
        name="ttt",
    )(*[pltpu.with_memory_space_constraint(a, pltpu.HBM) for a in (
        key_vectors, value_vectors, queries, step_sizes.T, fast_weights, fast_gain, window_gain
    )])
    return pl.pallas_call(
        finish,
        out_shape=(
            jax.ShapeDtypeStruct(queries.shape, BF16),
            jax.ShapeDtypeStruct(fast_weights.shape, F32),
            jax.ShapeDtypeStruct(fast_weights.shape, F32),
        ),
        in_specs=[vmem] * 3,
        out_specs=(hbm, hbm, hbm),
        scratch_shapes=[dma((3,))],
        compiler_params=pltpu.CompilerParams(vmem_limit_bytes=12 << 20),
        name="finish",
    )(*results)


def solution(mesh):
    in_specs = (
        P(("groups", "seq"), None),
        P(("groups", "seq"), None),
        P(("groups", "seq"), None),
        P(("groups", "seq"), None),
        P("seq", None),
        P(),
        P(),
    )
    out_specs = (P(("groups", "seq"), None), P(("groups", "seq"), None), P(("groups", "seq"), None))
    return jax.shard_map(shards, mesh=mesh, in_specs=in_specs, out_specs=out_specs, check_vma=False)
```
